32 devices in a mesh: seq: 16 (over z, y, core), tp: 2 (over x).
Axes of the slice: x: 2, y: 2, z: 4, core: 2. Of those that a mesh axis runs over, the one named last changes fastest.
Arguments:
- layer_input: bfloat16 [8192, 1792], P('seq'), may hold values from -6 to 6
- grad_output: bfloat16 [8192, 1792], P('seq'), may hold values from -6 to 6
- tile_image: int32 [64], replicated, may hold values from 0 to 63, as said below
- qkv_weight: bfloat16 [1792, 3, 1792], P('seq', None, 'tp'), may hold values from -0.125 to 0.125
- out_weight: bfloat16 [1792, 1792], P('seq', 'tp'), may hold values from -0.125 to 0.125
Outputs:
- grad_input: bfloat16 [8192, 1792], P('seq')
- qkv_grad: float32 [1792, 3, 1792], P('seq', None, 'tp')
- out_grad: float32 [1792, 1792], P('seq', 'tp')
The draws below stay inside these ranges and needn't reach their ends.
Inputs may be any that keep to these rules, and one draw needn't show every extreme that they name: `tile_image`: each image covers 1 to 4 consecutive whole tiles, and one covers exactly 4; an image's number is the index of its first tile, so numbers never fall along the tiles and the last tile is an image of its own; every boundary between the tiles of two consecutive seq shards lies inside an image, which covers 1 or 2 tiles on each side of it.
All inputs are finite; a program needn't handle non-finite values.
Results may differ from the reference program's by a relative error of at most 0.025.
Values may be sent and summed in bfloat16 or wider, within the bound.
No kernel may reach another device: no remote copies, remote signals or barrier semaphores. Data moves between devices by JAX's collectives and lax.ppermute only.
A program may use at most 128 MiB of HBM per device.

```python
import jax
import jax.numpy as jnp
from jax import lax

D = 1792
HEADS = 16
HD = 112
TILE = 128
MOST = 4
RIM = 384
TOK_DEV = 512
TOKENS = 8192
NTILES = 64


def draw_tile_image(key, part):
    per_shard = TOK_DEV // TILE
    shards = NTILES // per_shard
    key_before, key_after, key_extra = jax.random.split(key, 3)
    before = jax.random.randint(key_before, (shards + 1,), 1, 3, dtype=jnp.int32)
    after = jax.random.randint(key_after, (shards,), 1, 3, dtype=jnp.int32)
    before = before.at[1].set(2).at[shards].set(0)
    after = after.at[1].set(2).at[0].set(0)
    tiles = jnp.arange(NTILES, dtype=jnp.int32)
    shard_of = tiles // per_shard
    position = tiles % per_shard
    lower = after[shard_of]
    upper = per_shard - before[shard_of + 1]
    extra = jax.random.randint(key_extra, (NTILES,), 0, 3, dtype=jnp.int32) == 0
    in_gap = (position >= lower) & (position < upper)
    starts = (position == lower) | (position == upper) | in_gap & (((position - lower) % MOST == 0) | extra)
    starts = starts | (tiles == NTILES - 1)
    firsts = jnp.where(starts, tiles, jnp.zeros_like(tiles))
    return lax.cummax(firsts, axis=0).astype(jnp.int32)


def spiked(values, rng, source, target, shards_of, factor):
    def block_of(axis_at):
        return (jnp.arange(values.shape[axis_at]) // (values.shape[axis_at] // shards_of)).reshape((-1,) + (1,) * (values.ndim - 1 - axis_at))

    one_side = jax.random.permutation(rng, shards_of)[block_of(target)]
    other_side = (block_of(target) + shards_of // 2) % shards_of
    return jnp.where((block_of(source) == one_side) | (block_of(source) == other_side), factor * values, values)


def block_levels(stream_key, extent, pieces, least, largest):
    loudness = 1.0
    for axis_at, blocks in pieces:
        steps = jax.random.uniform(jax.random.fold_in(jax.random.fold_in(stream_key, 6), axis_at), (blocks,), jnp.float32, least / len(pieces), largest / len(pieces))
        loudness = loudness * jnp.repeat(jnp.exp(steps), extent[axis_at] // blocks).reshape((-1,) + (1,) * (len(extent) - 1 - axis_at))
    return loudness


def bell_draw(own_key, shape, spread, most, pieces=(), kind=jnp.bfloat16):
    array = jax.random.normal(own_key, shape, jnp.float32) * spread
    if len(pieces) > 0:
        array = block_levels(own_key, shape, pieces, -0.22, 0.18) * array
    return jnp.clip(array, min=-most, max=most).astype(kind)


def bell_draw_with(rng, extent, width, bound, cuts, heavy, kind=jnp.bfloat16):
    array = width * jax.random.normal(rng, extent, jnp.float32)
    if cuts:
        array = array * block_levels(rng, extent, cuts, -0.22, 0.18)
    return jnp.clip(spiked(array, jax.random.fold_in(rng, 3), *heavy), -bound, bound).astype(kind)


def setup_inputs(seed: int = 0) -> dict:
    seeds = jax.random.split(jax.random.key(seed), 6)
    return {
        "layer_input": bell_draw(seeds[0], (TOKENS, D), 1.0, 6.0, ((0, 16),)),
        "grad_output": bell_draw_with(seeds[1], (TOKENS, D), 1.0, 6.0, ((0, 16),), (0, 1, 16, 2.0)),
        "tile_image": draw_tile_image(jax.random.fold_in(seeds[5], 71), 0),
        "qkv_weight": bell_draw(seeds[3], (D, 3, D), D ** -0.5, 0.125, ((0, 16), (2, 2))),
        "out_weight": bell_draw(seeds[4], (D, D), D ** -0.5, 0.125, ((0, 16), (1, 2))),
    }


def attend_block(queries, key_rows, value_rows, upstream, query_ids, key_ids, factor):
    scores = jnp.einsum('qhd,khd->hqk', queries.astype(jnp.float32), key_rows.astype(jnp.float32)) * factor
    allowed = query_ids[:, None] == key_ids[None, :]
    exponent = jnp.where(allowed, jnp.exp(scores), 0.0)
    attn_prob = exponent / lax.optimization_barrier(jnp.sum(exponent, axis=-1, keepdims=True))
    prob_low = attn_prob.astype(jnp.bfloat16)
    attended = jnp.einsum('hqk,khd->qhd', prob_low.astype(jnp.float32), value_rows.astype(jnp.float32))
    up_float = upstream.astype(jnp.float32)
    dprob = jnp.einsum('qhd,khd->hqk', up_float, value_rows.astype(jnp.float32))
    row_delta = jnp.einsum('qhd,qhd->hq', up_float, attended)[:, :, None]
    dscore = (attn_prob * (dprob - row_delta) * factor).astype(jnp.bfloat16)
    dscore_f = dscore.astype(jnp.float32)
    dquery = jnp.einsum('hqk,khd->qhd', dscore_f, key_rows.astype(jnp.float32)).astype(jnp.bfloat16)
    dkey = jnp.einsum('hqk,qhd->khd', dscore_f, queries.astype(jnp.float32))
    dvalue = jnp.einsum('hqk,qhd->khd', prob_low.astype(jnp.float32), up_float)
    return (attended.astype(jnp.bfloat16), dquery, dkey, dvalue)

def reference(layer_input, grad_output, tile_image, qkv_weight, out_weight):
    widened = layer_input.astype(jnp.float32)
    center = widened - lax.optimization_barrier(jnp.mean(widened, axis=-1, keepdims=True))
    inv_std = lax.rsqrt(lax.optimization_barrier(jnp.mean(center * center, axis=-1, keepdims=True)) + 1e-06)
    normed = center * inv_std
    normed_low = normed.astype(jnp.bfloat16)
    projected = jnp.einsum('td,dce->cte', normed_low.astype(jnp.float32), qkv_weight.astype(jnp.float32)).astype(jnp.bfloat16)
    upstream = jnp.dot(grad_output, out_weight, preferred_element_type=jnp.float32).astype(jnp.bfloat16)
    query_heads = projected[0].reshape(TOKENS, HEADS, HD)
    key_pad = jnp.pad(projected[1].reshape(TOKENS, HEADS, HD), ((RIM, RIM), (0, 0), (0, 0)))
    value_pad = jnp.pad(projected[2].reshape(TOKENS, HEADS, HD), ((RIM, RIM), (0, 0), (0, 0)))
    up_heads = upstream.reshape(TOKENS, HEADS, HD)
    all_ids = jnp.repeat(jnp.pad(tile_image, (MOST - 1, MOST - 1), constant_values=-1), TILE)
    block_rows = min(TOK_DEV, 512)
    reach = block_rows + 2 * RIM
    factor = float(HD) ** (-0.5)

    def step(carry, block):
        grad_keys, grad_values = carry
        first = (block * block_rows).astype(jnp.int32)
        queries = lax.dynamic_slice_in_dim(query_heads, first, block_rows, 0)
        key_rows = lax.dynamic_slice_in_dim(key_pad, first, reach, 0)
        value_rows = lax.dynamic_slice_in_dim(value_pad, first, reach, 0)
        up_rows = lax.dynamic_slice_in_dim(up_heads, first, block_rows, 0)
        query_ids = lax.dynamic_slice_in_dim(all_ids, first + RIM, block_rows, 0)
        key_ids = lax.dynamic_slice_in_dim(all_ids, first, reach, 0)
        attended, dquery, dkey, dvalue = attend_block(queries, key_rows, value_rows, up_rows, query_ids, key_ids, factor)
        old_keys = lax.dynamic_slice_in_dim(grad_keys, first, reach, 0)
        old_values = lax.dynamic_slice_in_dim(grad_values, first, reach, 0)
        grad_keys = lax.dynamic_update_slice_in_dim(grad_keys, old_keys + dkey, first, 0)
        grad_values = lax.dynamic_update_slice_in_dim(grad_values, old_values + dvalue, first, 0)
        return ((grad_keys, grad_values), (attended, dquery))
    start_keys = jnp.zeros((TOKENS + 2 * RIM, HEADS, HD), jnp.float32)
    start_values = jnp.zeros((TOKENS + 2 * RIM, HEADS, HD), jnp.float32)
    (grad_keys, grad_values), (attended_all, dquery_all) = lax.scan(step, (start_keys, start_values), jnp.arange(TOKENS // block_rows, dtype=jnp.int32))
    attended_low = attended_all.reshape(TOKENS, D)
    dquery_low = dquery_all.reshape(TOKENS, D)
    dkey_low = grad_keys[RIM:RIM + TOKENS].reshape(TOKENS, D).astype(jnp.bfloat16)
    dvalue_low = grad_values[RIM:RIM + TOKENS].reshape(TOKENS, D).astype(jnp.bfloat16)
    grad_proj = jnp.stack([dquery_low, dkey_low, dvalue_low], axis=1)
    grad_float = grad_proj.astype(jnp.float32)
    qkv_grad = jnp.einsum('td,tce->dce', normed_low.astype(jnp.float32), grad_float)
    out_grad = jnp.dot(grad_output.T, attended_low, preferred_element_type=jnp.float32)
    grad_norm = jnp.einsum('tce,dce->td', grad_float, qkv_weight.astype(jnp.float32))
    grad_input = inv_std * (grad_norm - lax.optimization_barrier(jnp.mean(grad_norm, axis=-1, keepdims=True)) - normed * lax.optimization_barrier(jnp.mean(grad_norm * normed, axis=-1, keepdims=True)))
    return (grad_input.astype(jnp.bfloat16), qkv_grad, out_grad)
```

```python
import jax
import jax.numpy as jnp
from jax import lax
from jax.sharding import PartitionSpec as P

HD = 112
TILE = 128
MOST = 4
HALO = 256


def rings(count):
    lines = count // 4
    core = [(s, s ^ 1) for s in range(count)]
    pair = [(s, s ^ 2) for s in range(count)]

    def turn(k):
        return [(s, (s - 4 * k) % count) for s in range(count)]

    return lines, core, pair, turn


def gather_rows(shard):
    lines, core, pair, turn = rings(lax.axis_size("seq"))
    blocks = [shard] + [lax.ppermute(shard, "seq", turn(k)) for k in range(1, lines)]
    line = jnp.concatenate(blocks, axis=0)
    across = lax.ppermute(line, "seq", pair)
    line_other = lax.ppermute(line, "seq", core)
    across_other = lax.ppermute(across, "seq", core)
    return jnp.concatenate([line, across, line_other, across_other], axis=0)


def scatter_rows(partial):
    lines, core, pair, turn = rings(lax.axis_size("seq"))
    half = partial.shape[0] // 2
    quarter = half // 2
    rows = quarter // lines
    low = jnp.bfloat16
    received = lax.ppermute(partial[half:].astype(low), "seq", core)
    mine = partial[:half] + received.astype(jnp.float32)
    received = lax.ppermute(mine[quarter:].astype(low), "seq", pair)
    line = mine[:quarter] + received.astype(jnp.float32)
    total = line[:rows]
    for k in range(1, lines):
        piece = line[rows * k : rows * (k + 1)].astype(low)
        total = total + lax.ppermute(piece, "seq", turn(lines - k)).astype(jnp.float32)
    return total


def order_matrix(rows):
    lines = lax.axis_size("seq") // 4
    me = lax.axis_index("seq")
    line, pair, core = me // 4, (me // 2) % 2, me % 2
    width = 4 * lines * rows
    place = lax.broadcasted_iota(jnp.int32, (width, width), 1)
    at = place // rows
    source = (
        ((line + at % lines) % lines) * 4
        + (pair ^ ((at // lines) % 2)) * 2
        + (core ^ (at // (2 * lines)))
    )
    wanted = source * rows + place % rows
    have = lax.broadcasted_iota(jnp.int32, (width, width), 0)
    return (have == wanted).astype(jnp.bfloat16)


def shift(block, distance):
    count = lax.axis_size("seq")
    route = [(i, i + distance) for i in range(count) if 0 <= i + distance < count]
    return lax.ppermute(block, "seq", route)


def layer_stats(layer_input):
    widened = layer_input.astype(jnp.float32)
    center = widened - jnp.mean(widened, axis=-1, keepdims=True)
    inv_std = lax.rsqrt(jnp.mean(center * center, axis=-1, keepdims=True) + 1e-06)
    return (center * inv_std, inv_std)


def norm_back(grad_norm, normed, inv_std):
    return inv_std * (
        grad_norm
        - jnp.mean(grad_norm, axis=-1, keepdims=True)
        - normed * jnp.mean(grad_norm * normed, axis=-1, keepdims=True)
    )


def attend_block(queries, key_rows, value_rows, upstream, query_ids, key_ids, factor):
    scores = (
        jnp.einsum("qhd,khd->hqk", queries, key_rows, preferred_element_type=jnp.float32) * factor
    )
    allowed = query_ids[:, None] == key_ids[None, :]
    exponent = jnp.where(allowed, jnp.exp(scores), 0.0)
    attn_prob = exponent / jnp.sum(exponent, axis=-1, keepdims=True)
    prob_low = attn_prob.astype(jnp.bfloat16)
    attended = jnp.einsum("hqk,khd->qhd", prob_low, value_rows, preferred_element_type=jnp.float32)
    dprob = jnp.einsum("qhd,khd->hqk", upstream, value_rows, preferred_element_type=jnp.float32)
    row_delta = jnp.einsum("qhd,qhd->hq", upstream.astype(jnp.float32), attended)[:, :, None]
    dscore = (attn_prob * (dprob - row_delta) * factor).astype(jnp.bfloat16)
    dquery = jnp.einsum(
        "hqk,khd->qhd", dscore, key_rows, preferred_element_type=jnp.float32
    ).astype(jnp.bfloat16)
    dkey = jnp.einsum("hqk,qhd->khd", dscore, queries, preferred_element_type=jnp.float32)
    dvalue = jnp.einsum("hqk,qhd->khd", prob_low, upstream, preferred_element_type=jnp.float32)
    return (attended.astype(jnp.bfloat16), dquery, dkey, dvalue)


def dot(a, b, contract):
    return lax.dot_general(
        a, b, ((contract[:1], contract[1:]), ((), ())), preferred_element_type=jnp.float32
    )


def per_device(layer_input, grad_output, tile_image, qkv_weight, out_weight):
    low = jnp.bfloat16
    seq_index = lax.axis_index("seq")
    tokens = layer_input.shape[0]
    own_rows, _, width = qkv_weight.shape
    heads = width // HD
    weights = [gather_rows(piece) for piece in (
        qkv_weight[:, 1], qkv_weight[:, 2], qkv_weight[:, 0], out_weight
    )]
    order = order_matrix(own_rows)
    normed, inv_std = layer_stats(dot(layer_input, order, (1, 0)).astype(low))
    normed_low = normed.astype(low)
    grad_out = dot(grad_output, order, (1, 0)).astype(low)
    key, value, query = [dot(normed_low, w, (1, 0)).astype(low) for w in weights[:3]]
    upstream = dot(grad_out, weights[3], (1, 0)).astype(low)
    pair = jnp.stack([key, value])
    padded = jnp.concatenate(
        [shift(pair[:, tokens - HALO :], 1), pair, shift(pair[:, :HALO], -1)], axis=1
    )
    span = tokens + 2 * HALO
    tiles_dev = tokens // TILE
    reach = HALO // TILE
    padded_ids = jnp.pad(tile_image, (reach, reach), constant_values=-1)
    window_ids = lax.dynamic_slice_in_dim(
        padded_ids, seq_index * tiles_dev, tiles_dev + 2 * reach, 0
    )
    key_ids = jnp.repeat(window_ids, TILE)
    attended, dquery, dkey, dvalue = attend_block(
        query.reshape(tokens, heads, HD),
        padded[0].reshape(span, heads, HD),
        padded[1].reshape(span, heads, HD),
        upstream.reshape(tokens, heads, HD),
        key_ids[HALO : HALO + tokens],
        key_ids,
        float(HD) ** (-0.5),
    )
    attended = attended.reshape(tokens, width)
    dquery = dquery.reshape(tokens, width)
    grads = jnp.stack([dkey, dvalue]).reshape(2, span, width)
    from_next = shift(grads[:, :HALO].astype(low), -1).astype(jnp.float32)
    from_prev = shift(grads[:, HALO + tokens :].astype(low), 1).astype(jnp.float32)
    own = grads[:, HALO : HALO + tokens]
    own = own.at[:, :HALO].add(from_prev).at[:, tokens - HALO :].add(from_next).astype(low)
    flat = [own[0], own[1], dquery]
    out_grad = scatter_rows(dot(grad_out, attended, (0, 0)))
    d_query = scatter_rows(dot(normed_low, dquery, (0, 0)))
    d_key = scatter_rows(dot(normed_low, own[0], (0, 0)))
    d_value = scatter_rows(dot(normed_low, own[1], (0, 0)))
    qkv_grad = jnp.stack([d_query, d_key, d_value], axis=1)
    grad_norm = sum(dot(g, w, (1, 1)) for g, w in zip(flat, weights[:3]))
    parts = lax.axis_size("tp")
    if parts == 2:
        ours = grad_norm.astype(low)
        theirs = lax.ppermute(ours, "tp", [(0, 1), (1, 0)])
        total = ours.astype(jnp.float32) + theirs.astype(jnp.float32)
        grad_input = norm_back(total, normed, inv_std).astype(low)
    else:
        share = tokens // parts
        first_row = lax.axis_index("tp") * share
        total = lax.psum_scatter(grad_norm, "tp", scatter_dimension=0, tiled=True)
        rows = lax.dynamic_slice_in_dim(normed, first_row, share, 0)
        scales = lax.dynamic_slice_in_dim(inv_std, first_row, share, 0)
        piece = norm_back(total, rows, scales).astype(low)
        grad_input = lax.all_gather(piece, "tp", axis=0, tiled=True)
    grad_input = dot(grad_input, order, (1, 1)).astype(low)
    return (grad_input, qkv_grad, out_grad)


def solution(mesh):
    placed = (P("seq", None), P("seq", None), P(), P("seq", None, "tp"), P("seq", "tp"))
    return jax.shard_map(
        per_device,
        mesh=mesh,
        in_specs=placed,
        out_specs=(P("seq", None), P("seq", None, "tp"), P("seq", "tp")),
        check_vma=False,
    )
```

```python
import math

import jax
import jax.numpy as jnp
from jax import lax
from jax.experimental import pallas as pl
from jax.experimental.pallas import tpu as pltpu
from jax.sharding import PartitionSpec as P

HD = 112
TILE = 128
MOST = 4
HALO = 256
LANES = 256


def rings(count):
    lines = count // 4
    core = [(s, s ^ 1) for s in range(count)]
    pair = [(s, s ^ 2) for s in range(count)]

    def turn(k):
        return [(s, (s - 4 * k) % count) for s in range(count)]

    return lines, core, pair, turn


def gather_rows(shards):
    lines, core, pair, turn = rings(lax.axis_size("seq"))
    gathered = []
    blocks = []
    for shard in shards:
        if blocks:
            shard, *blocks = lax.optimization_barrier((shard, *blocks))
        blocks = [lax.ppermute(shard, "seq", turn(k)) for k in range(1, lines)]
        line = jnp.concatenate([shard, *blocks], axis=0)
        across = lax.ppermute(line, "seq", pair)
        line_other = lax.ppermute(line, "seq", core)
        across_other = lax.ppermute(across, "seq", core)
        gathered.append(jnp.concatenate([line, across, line_other, across_other], axis=0))
    return gathered


def scatter_rows(partial):
    lines, core, pair, turn = rings(lax.axis_size("seq"))
    half = partial.shape[0] // 2
    quarter = half // 2
    rows = quarter // lines
    low = jnp.bfloat16
    received = lax.ppermute(partial[half:].astype(low), "seq", core)
    mine = partial[:half] + received.astype(jnp.float32)
    received = lax.ppermute(mine[quarter:].astype(low), "seq", pair)
    line = mine[:quarter] + received.astype(jnp.float32)
    total = line[:rows]
    for k in range(1, lines):
        piece = line[rows * k : rows * (k + 1)].astype(low)
        total = total + lax.ppermute(piece, "seq", turn(lines - k)).astype(jnp.float32)
    return total


def order_matrix(rows):
    lines = lax.axis_size("seq") // 4
    me = lax.axis_index("seq")
    line, pair, core = me // 4, (me // 2) % 2, me % 2
    width = 4 * lines * rows
    place = lax.broadcasted_iota(jnp.int32, (width, width), 1)
    at = place // rows
    source = (
        ((line + at % lines) % lines) * 4
        + (pair ^ ((at // lines) % 2)) * 2
        + (core ^ (at // (2 * lines)))
    )
    wanted = source * rows + place % rows
    have = lax.broadcasted_iota(jnp.int32, (width, width), 0)
    return (have == wanted).astype(jnp.bfloat16)


def shift(block, distance):
    count = lax.axis_size("seq")
    route = [(i, i + distance) for i in range(count) if 0 <= i + distance < count]
    return lax.ppermute(block, "seq", route)


def layer_stats(layer_input):
    widened = layer_input.astype(jnp.float32)
    center = widened - jnp.mean(widened, axis=-1, keepdims=True)
    inv_std = lax.rsqrt(jnp.mean(center * center, axis=-1, keepdims=True) + 1e-06)
    return (center * inv_std, inv_std)


def norm_back(grad_norm, normed, inv_std):
    return inv_std * (
        grad_norm
        - jnp.mean(grad_norm, axis=-1, keepdims=True)
        - normed * jnp.mean(grad_norm * normed, axis=-1, keepdims=True)
    )


def dot(a, b, contract):
    return lax.dot_general(
        a, b, ((contract[:1], contract[1:]), ((), ())), preferred_element_type=jnp.float32
    )


def attend_kernel(
    ids, starts, q_ref, u_ref, k_ref, v_ref, before, after,
    att_ref, dq_ref, dk_ref, dv_ref, dbefore, dafter,
    qs, us, ks, vs, gk, gv, at, dqs,
):
    low = jnp.bfloat16
    tokens, width = q_ref.shape
    halo = before.shape[1]
    reach = halo // TILE
    keys = MOST * TILE
    factor = float(HD) ** (-0.5)
    pair_width = 2 * HD
    first = lax.broadcasted_iota(jnp.int32, (1, LANES), 1) < HD
    for pair in range(width // pair_width):
        cols = slice(pair_width * pair, pair_width * (pair + 1))

        def spread(target, row, block):
            rows = slice(row, row + block.shape[0])
            target[rows, :pair_width] = block
            target[rows, pair_width:] = jnp.zeros((block.shape[0], LANES - pair_width), low)

        spread(qs, 0, q_ref[:, cols])
        spread(us, 0, u_ref[:, cols])
        for target, own, at_side in ((ks, k_ref, 0), (vs, v_ref, 1)):
            spread(target, 0, before[at_side, :, cols])
            spread(target, halo, own[:, cols])
            spread(target, halo + tokens, after[at_side, :, cols])
        gk[...] = jnp.zeros(gk.shape, jnp.float32)
        gv[...] = jnp.zeros(gv.shape, jnp.float32)
        for i in range(tokens // TILE):
            rows = slice(i * TILE, (i + 1) * TILE)
            start = starts[i]
            window = pl.ds(pl.multiple_of(start * TILE, TILE), keys)
            image = ids[i + reach]
            q, u = qs[rows, :], us[rows, :]
            zero = jnp.zeros_like(q)
            both_q = jnp.concatenate([jnp.where(first, q, zero), jnp.where(first, zero, q)], axis=0)
            both_u = jnp.concatenate([jnp.where(first, u, zero), jnp.where(first, zero, u)], axis=0)
            k, v = ks[window, :], vs[window, :]
            scores = dot(k, both_q, (1, 1)) * (factor * math.log2(math.e))
            dprob = dot(v, both_u, (1, 1))
            exponent = jnp.concatenate(
                [
                    jnp.where(
                        ids[start + j] == image, jnp.exp2(scores[j * TILE : (j + 1) * TILE]), 0.0
                    )
                    for j in range(MOST)
                ],
                axis=0,
            )
            prob = exponent / jnp.sum(exponent, axis=0, keepdims=True)
            prob_low = prob.astype(low)
            delta = jnp.sum(prob_low.astype(jnp.float32) * dprob, axis=0, keepdims=True)
            dscore = (prob * (dprob - delta) * factor).astype(low)
            out = dot(prob_low, v, (0, 0))
            at[rows, :] = jnp.where(first, out[:TILE], out[TILE:]).astype(low)
            out = dot(dscore, k, (0, 0))
            dqs[rows, :] = jnp.where(first, out[:TILE], out[TILE:]).astype(low)
            gv[window, :] += dot(prob_low, both_u, (1, 0))
            gk[window, :] += dot(dscore, both_q, (1, 0))
        att_ref[:, cols] = at[:, :pair_width]
        dq_ref[:, cols] = dqs[:, :pair_width]
        for source, own, at_side in ((gk, dk_ref, 0), (gv, dv_ref, 1)):
            dbefore[at_side, :, cols] = source[:halo, :pair_width].astype(low)
            own[:, cols] = source[halo : halo + tokens, :pair_width].astype(low)
            dafter[at_side, :, cols] = source[halo + tokens :, :pair_width].astype(low)


def attend(ids, starts, query, upstream, key, value, before, after):
    low = jnp.bfloat16
    tokens = query.shape[0]
    span = tokens + 2 * before.shape[1]
    results = (query, query, key, value, before, after)
    return pl.pallas_call(
        attend_kernel,
        in_specs=[pl.BlockSpec(memory_space=pltpu.SMEM)] * 2
        + [pl.BlockSpec(memory_space=pltpu.VMEM)] * 6,
        out_specs=[pl.BlockSpec(memory_space=pltpu.VMEM)] * 6,
        out_shape=[jax.ShapeDtypeStruct(x.shape, low) for x in results],
        scratch_shapes=[pltpu.VMEM((tokens, LANES), low)] * 2
        + [pltpu.VMEM((span, LANES), low)] * 2
        + [pltpu.VMEM((span, LANES), jnp.float32)] * 2
        + [pltpu.VMEM((tokens, LANES), low)] * 2,
        name="attend",
    )(ids, starts, query, upstream, key, value, before, after)


def per_device(layer_input, grad_output, tile_image, qkv_weight, out_weight):
    low = jnp.bfloat16
    seq_index = lax.axis_index("seq")
    tokens = layer_input.shape[0]
    own_rows, _, width = qkv_weight.shape
    weights = gather_rows((qkv_weight[:, 1], qkv_weight[:, 2], qkv_weight[:, 0], out_weight))
    order = order_matrix(own_rows)
    normed, inv_std = layer_stats(dot(layer_input, order, (1, 0)).astype(low))
    normed_low = normed.astype(low)
    grad_out = dot(grad_output, order, (1, 0)).astype(low)
    key, value, query = [dot(normed_low, w, (1, 0)).astype(low) for w in weights[:3]]
    upstream = dot(grad_out, weights[3], (1, 0)).astype(low)
    before = shift(jnp.stack([key[tokens - HALO :], value[tokens - HALO :]]), 1)
    after = shift(jnp.stack([key[:HALO], value[:HALO]]), -1)
    tiles_dev = tokens // TILE
    reach = HALO // TILE
    base = seq_index * tiles_dev
    padded_ids = jnp.pad(tile_image, (reach, reach), constant_values=-1)
    ids = lax.dynamic_slice_in_dim(padded_ids, base, tiles_dev + 2 * reach, 0)
    starts = jnp.clip(
        ids[reach : reach + tiles_dev] - base + reach, 0, tiles_dev + 2 * reach - MOST
    )
    attended, dquery, dkey, dvalue, dbefore, dafter = attend(
        ids, starts, query, upstream, key, value, before, after
    )
    edge = tokens - HALO
    from_next = shift(dbefore, -1)
    from_prev = shift(dafter, 1)
    own = []
    for side, grad in enumerate((dkey, dvalue)):
        grad = grad.astype(jnp.float32)
        grad = grad + jnp.pad(from_prev[side].astype(jnp.float32), ((0, edge), (0, 0)))
        grad = grad + jnp.pad(from_next[side].astype(jnp.float32), ((edge, 0), (0, 0)))
        own.append(grad.astype(low))
    out_grad = scatter_rows(dot(grad_out, attended, (0, 0)))
    d_query = scatter_rows(dot(normed_low, dquery, (0, 0)))
    d_key = scatter_rows(dot(normed_low, own[0], (0, 0)))
    d_value = scatter_rows(dot(normed_low, own[1], (0, 0)))
    qkv_grad = jnp.stack([d_query, d_key, d_value], axis=1)
    grad_norm = sum(dot(g, w, (1, 1)) for g, w in zip((*own, dquery), weights[:3]))
    parts = lax.axis_size("tp")
    if parts == 2:
        ours = grad_norm.astype(low)
        theirs = lax.ppermute(ours, "tp", [(0, 1), (1, 0)])
        total = ours.astype(jnp.float32) + theirs.astype(jnp.float32)
        grad_input = norm_back(total, normed, inv_std).astype(low)
    else:
        share = tokens // parts
        first_row = lax.axis_index("tp") * share
        total = lax.psum_scatter(grad_norm, "tp", scatter_dimension=0, tiled=True)
        rows = lax.dynamic_slice_in_dim(normed, first_row, share, 0)
        scales = lax.dynamic_slice_in_dim(inv_std, first_row, share, 0)
        piece = norm_back(total, rows, scales).astype(low)
        grad_input = lax.all_gather(piece, "tp", axis=0, tiled=True)
    grad_input = dot(grad_input, order, (1, 1)).astype(low)
    return (grad_input, qkv_grad, out_grad)


def solution(mesh):
    placed = (P("seq", None), P("seq", None), P(), P("seq", None, "tp"), P("seq", "tp"))
    return jax.shard_map(
        per_device,
        mesh=mesh,
        in_specs=placed,
        out_specs=(P("seq", None), P("seq", None, "tp"), P("seq", "tp")),
        check_vma=False,
    )
```

```python
import math

import jax
import jax.numpy as jnp
from jax import lax
from jax.experimental import pallas as pl
from jax.experimental.pallas import tpu as pltpu
from jax.sharding import PartitionSpec as P

HD = 112
TILE = 128
MOST = 4
HALO = 256
LANES = 256


def rings(count):
    lines = count // 4
    core = [(s, s ^ 1) for s in range(count)]
    pair = [(s, s ^ 2) for s in range(count)]

    def turn(k):
        return [(s, (s - 4 * k) % count) for s in range(count)]

    return lines, core, pair, turn


def gather_rows(shards):
    lines, core, pair, turn = rings(lax.axis_size("seq"))
    gathered = []
    blocks = []
    for shard in shards:
        if blocks:
            shard, *blocks = lax.optimization_barrier((shard, *blocks))
        blocks = [lax.ppermute(shard, "seq", turn(k)) for k in range(1, lines)]
        line = jnp.concatenate([shard, *blocks], axis=0)
        across = lax.ppermute(line, "seq", pair)
        line_other = lax.ppermute(line, "seq", core)
        across_other = lax.ppermute(across, "seq", core)
        gathered.append(jnp.concatenate([line, across, line_other, across_other], axis=0))
    return gathered


def scatter_rows(partial):
    lines, core, pair, turn = rings(lax.axis_size("seq"))
    half = partial.shape[0] // 2
    quarter = half // 2
    rows = quarter // lines
    low = jnp.bfloat16
    received = lax.ppermute(partial[half:].astype(low), "seq", core)
    mine = partial[:half] + received.astype(jnp.float32)
    received = lax.ppermute(mine[quarter:].astype(low), "seq", pair)
    line = mine[:quarter] + received.astype(jnp.float32)
    total = line[:rows]
    for k in range(1, lines):
        piece = line[rows * k : rows * (k + 1)].astype(low)
        total = total + lax.ppermute(piece, "seq", turn(lines - k)).astype(jnp.float32)
    return total


def order_matrix(rows):
    lines = lax.axis_size("seq") // 4
    me = lax.axis_index("seq")
    line, pair, core = me // 4, (me // 2) % 2, me % 2
    width = 4 * lines * rows
    place = lax.broadcasted_iota(jnp.int32, (width, width), 1)
    at = place // rows
    source = (
        ((line + at % lines) % lines) * 4
        + (pair ^ ((at // lines) % 2)) * 2
        + (core ^ (at // (2 * lines)))
    )
    wanted = source * rows + place % rows
    have = lax.broadcasted_iota(jnp.int32, (width, width), 0)
    return (have == wanted).astype(jnp.bfloat16)


def shift(block, distance):
    count = lax.axis_size("seq")
    route = [(i, i + distance) for i in range(count) if 0 <= i + distance < count]
    return lax.ppermute(block, "seq", route)


def layer_stats(layer_input):
    widened = layer_input.astype(jnp.float32)
    center = widened - jnp.mean(widened, axis=-1, keepdims=True)
    inv_std = lax.rsqrt(jnp.mean(center * center, axis=-1, keepdims=True) + 1e-06)
    return (center * inv_std, inv_std)


def norm_back(grad_norm, normed, inv_std):
    return inv_std * (
        grad_norm
        - jnp.mean(grad_norm, axis=-1, keepdims=True)
        - normed * jnp.mean(grad_norm * normed, axis=-1, keepdims=True)
    )


def dot(a, b, contract):
    return lax.dot_general(
        a, b, ((contract[:1], contract[1:]), ((), ())), preferred_element_type=jnp.float32
    )


def attend_kernel(
    ids, starts, q_ref, u_ref, kv_ref, before, after,
    att_ref, dq_ref, dkv_ref, dbefore, dafter,
    qs, us, ks, vs, gk, gv, at, dqs,
):
    low = jnp.bfloat16
    tokens, width = q_ref.shape
    halo = before.shape[0]
    reach = halo // TILE
    keys = MOST * TILE
    factor = float(HD) ** (-0.5)
    pair_width = 2 * HD
    first = lax.broadcasted_iota(jnp.int32, (1, LANES), 1) < HD
    for pair in range(width // pair_width):
        cols = slice(pair_width * pair, pair_width * (pair + 1))
        value_cols = slice(width + cols.start, width + cols.stop)

        def spread(target, row, block):
            rows = slice(row, row + block.shape[0])
            target[rows, :pair_width] = block
            target[rows, pair_width:] = jnp.zeros((block.shape[0], LANES - pair_width), low)

        spread(qs, 0, q_ref[:, cols])
        spread(us, 0, u_ref[:, cols])
        for target, source_cols in ((ks, cols), (vs, value_cols)):
            spread(target, 0, before[:, source_cols])
            spread(target, halo, kv_ref[:, source_cols])
            spread(target, halo + tokens, after[:, source_cols])
        gk[...] = jnp.zeros(gk.shape, jnp.float32)
        gv[...] = jnp.zeros(gv.shape, jnp.float32)
        for i in range(tokens // TILE):
            rows = slice(i * TILE, (i + 1) * TILE)
            start = starts[i]
            window = pl.ds(pl.multiple_of(start * TILE, TILE), keys)
            image = ids[i + reach]
            q, u = qs[rows, :], us[rows, :]
            zero = jnp.zeros_like(q)
            both_q = jnp.concatenate([jnp.where(first, q, zero), jnp.where(first, zero, q)], axis=0)
            both_u = jnp.concatenate([jnp.where(first, u, zero), jnp.where(first, zero, u)], axis=0)
            k, v = ks[window, :], vs[window, :]
            scores = dot(k, both_q, (1, 1)) * (factor * math.log2(math.e))
            dprob = dot(v, both_u, (1, 1))
            exponent = jnp.concatenate(
                [
                    jnp.where(
                        ids[start + j] == image, jnp.exp2(scores[j * TILE : (j + 1) * TILE]), 0.0
                    )
                    for j in range(MOST)
                ],
                axis=0,
            )
            prob = exponent / jnp.sum(exponent, axis=0, keepdims=True)
            prob_low = prob.astype(low)
            delta = jnp.sum(prob_low.astype(jnp.float32) * dprob, axis=0, keepdims=True)
            dscore = (prob * (dprob - delta) * factor).astype(low)
            out = dot(prob_low, v, (0, 0))
            at[rows, :] = jnp.where(first, out[:TILE], out[TILE:]).astype(low)
            out = dot(dscore, k, (0, 0))
            dqs[rows, :] = jnp.where(first, out[:TILE], out[TILE:]).astype(low)
            gv[window, :] += dot(prob_low, both_u, (1, 0))
            gk[window, :] += dot(dscore, both_q, (1, 0))
        att_ref[:, cols] = at[:, :pair_width]
        dq_ref[:, cols] = dqs[:, :pair_width]
        for source, target_cols in ((gk, cols), (gv, value_cols)):
            dbefore[:, target_cols] = source[:halo, :pair_width].astype(low)
            dkv_ref[:, target_cols] = source[halo : halo + tokens, :pair_width].astype(low)
            dafter[:, target_cols] = source[halo + tokens :, :pair_width].astype(low)


def attend(ids, starts, query, upstream, key_value, before, after):
    low = jnp.bfloat16
    tokens = query.shape[0]
    span = tokens + 2 * before.shape[0]
    results = (query, query, key_value, before, after)
    return pl.pallas_call(
        attend_kernel,
        in_specs=[pl.BlockSpec(memory_space=pltpu.SMEM)] * 2
        + [pl.BlockSpec(memory_space=pltpu.VMEM)] * 5,
        out_specs=[pl.BlockSpec(memory_space=pltpu.VMEM)] * 5,
        out_shape=[jax.ShapeDtypeStruct(x.shape, low) for x in results],
        scratch_shapes=[pltpu.VMEM((tokens, LANES), low)] * 2
        + [pltpu.VMEM((span, LANES), low)] * 2
        + [pltpu.VMEM((span, LANES), jnp.float32)] * 2
        + [pltpu.VMEM((tokens, LANES), low)] * 2,
        name="attend",
    )(ids, starts, query, upstream, key_value, before, after)


def per_device(layer_input, grad_output, tile_image, qkv_weight, out_weight):
    low = jnp.bfloat16
    tokens = layer_input.shape[0]
    own_rows, width = out_weight.shape
    groups = 2 if width % (4 * HD) == 0 else 1
    part = width // groups
    cuts = [slice(part * g, part * (g + 1)) for g in range(groups)]
    shards = []
    for cut in cuts:
        shards.append(jnp.concatenate([qkv_weight[:, 1, cut], qkv_weight[:, 2, cut]], axis=1))
        shards.append(jnp.concatenate([qkv_weight[:, 0, cut], out_weight[:, cut]], axis=1))
    weights = gather_rows(shards)
    order = order_matrix(own_rows)
    normed, inv_std = layer_stats(dot(layer_input, order, (1, 0)).astype(low))
    normed_low = normed.astype(low)
    grad_out = dot(grad_output, order, (1, 0)).astype(low)
    tiles_dev = tokens // TILE
    reach = HALO // TILE
    base = lax.axis_index("seq") * tiles_dev
    padded_ids = jnp.pad(tile_image, (reach, reach), constant_values=-1)
    ids = lax.dynamic_slice_in_dim(padded_ids, base, tiles_dev + 2 * reach, 0)
    starts = jnp.clip(
        ids[reach : reach + tiles_dev] - base + reach, 0, tiles_dev + 2 * reach - MOST
    )
    edge = tokens - HALO
    grad_norm = 0.0
    sums = []
    for kv_weight, qo_weight in zip(weights[::2], weights[1::2]):
        key_value = dot(normed_low, kv_weight, (1, 0)).astype(low)
        before = shift(key_value[edge:], 1)
        after = shift(key_value[:HALO], -1)
        query = dot(normed_low, qo_weight[:, :part], (1, 0)).astype(low)
        upstream = dot(grad_out, qo_weight[:, part:], (1, 0)).astype(low)
        attended, dquery, dkv, dbefore, dafter = attend(
            ids, starts, query, upstream, key_value, before, after
        )
        from_next = shift(dbefore, -1).astype(jnp.float32)
        from_prev = shift(dafter, 1).astype(jnp.float32)
        qo_part = [dot(normed_low, dquery, (0, 0)), dot(grad_out, attended, (0, 0))]
        qo_sum = scatter_rows(jnp.concatenate(qo_part, axis=1))
        dkv = dkv.astype(jnp.float32)
        dkv = dkv + jnp.pad(from_prev, ((0, edge), (0, 0)))
        dkv = (dkv + jnp.pad(from_next, ((edge, 0), (0, 0)))).astype(low)
        kv_sum = scatter_rows(dot(normed_low, dkv, (0, 0)))
        sums.append((qo_sum[:, :part], kv_sum[:, :part], kv_sum[:, part:], qo_sum[:, part:]))
        grad_norm = grad_norm + dot(dkv, kv_weight, (1, 1))
        grad_norm = grad_norm + dot(dquery, qo_weight[:, :part], (1, 1))
    d_query, d_key, d_value, out_grad = [jnp.concatenate(x, axis=1) for x in zip(*sums)]
    qkv_grad = jnp.stack([d_query, d_key, d_value], axis=1)
    parts = lax.axis_size("tp")
    if parts == 2:
        ours = grad_norm.astype(low)
        theirs = lax.ppermute(ours, "tp", [(0, 1), (1, 0)])
        total = ours.astype(jnp.float32) + theirs.astype(jnp.float32)
        grad_input = norm_back(total, normed, inv_std).astype(low)
    else:
        share = tokens // parts
        first_row = lax.axis_index("tp") * share
        total = lax.psum_scatter(grad_norm, "tp", scatter_dimension=0, tiled=True)
        rows = lax.dynamic_slice_in_dim(normed, first_row, share, 0)
        scales = lax.dynamic_slice_in_dim(inv_std, first_row, share, 0)
        piece = norm_back(total, rows, scales).astype(low)
        grad_input = lax.all_gather(piece, "tp", axis=0, tiled=True)
    grad_input = dot(grad_input, order, (1, 1)).astype(low)
    return (grad_input, qkv_grad, out_grad)


def solution(mesh):
    placed = (P("seq", None), P("seq", None), P(), P("seq", None, "tp"), P("seq", "tp"))
    return jax.shard_map(
        per_device,
        mesh=mesh,
        in_specs=placed,
        out_specs=(P("seq", None), P("seq", None, "tp"), P("seq", "tp")),
        check_vma=False,
    )
```

```python
import math

import jax
import jax.numpy as jnp
from jax import lax
from jax.experimental import pallas as pl
from jax.experimental.pallas import tpu as pltpu
from jax.sharding import PartitionSpec as P


HD = 112
TILE = 128
MOST = 4
HALO = 256
LANES = 256


def rings(count):
    lines = count // 4
    core = [(s, s ^ 1) for s in range(count)]
    pair = [(s, s ^ 2) for s in range(count)]

    def turn(k):
        return [(s, (s - 4 * k) % count) for s in range(count)]

    return lines, core, pair, turn


def send(block, route, axis="seq"):
    return lax.ppermute(block, axis, route)


def gather_rows(shards):
    lines, core, pair, turn = rings(lax.axis_size("seq"))
    gathered = {}
    blocks = []
    for name, shard in shards.items():
        if blocks:
            shard, *blocks = lax.optimization_barrier((shard, *blocks))
        blocks = [send(shard, turn(k)) for k in range(1, lines)]
        line = jnp.concatenate([shard, *blocks], axis=0)
        across = send(line, pair)
        half = jnp.concatenate([line, across], axis=0)
        gathered[name] = (half, send(half, core))
    return gathered


def scatter_far(rows_side, cols_side):
    _, core, _, _ = rings(lax.axis_size("seq"))
    half = rows_side.shape[1] // 2
    block = dot(rows_side[:, half:], cols_side, (0, 0)).astype(jnp.bfloat16)
    return block, send(block, core)


def scatter_near(rows_side, cols_side, far):
    _, _, pair, _ = rings(lax.axis_size("seq"))
    half = far.shape[0]
    quarter = half // 2
    near = dot(rows_side[:, quarter:half], cols_side, (0, 0)) + far[quarter:].astype(jnp.float32)
    near = near.astype(jnp.bfloat16)
    return near, send(near, pair)


def scatter_line(rows_side, cols_side, far, across):
    lines, _, _, turn = rings(lax.axis_size("seq"))
    low, wide = jnp.bfloat16, jnp.float32
    quarter = across.shape[0]
    rows = quarter // lines
    line = dot(rows_side[:, :quarter], cols_side, (0, 0)) + far[:quarter].astype(wide)
    line = (line + across.astype(wide)).astype(low)
    blocks = [line[:rows]]
    for k in range(1, lines):
        piece = line[rows * k : rows * (k + 1)]
        blocks.append(send(piece, turn(lines - k)))
    return line, blocks


def order_matrix(rows):
    lines = lax.axis_size("seq") // 4
    me = lax.axis_index("seq")
    line, pair, core = me // 4, (me // 2) % 2, me % 2
    width = 4 * lines * rows
    place = lax.broadcasted_iota(jnp.int32, (width, width), 1)
    at = place // rows
    source = (
        ((line + at % lines) % lines) * 4
        + (pair ^ ((at // lines) % 2)) * 2
        + (core ^ (at // (2 * lines)))
    )
    wanted = source * rows + place % rows
    have = lax.broadcasted_iota(jnp.int32, (width, width), 0)
    return (have == wanted).astype(jnp.bfloat16)


def layer_stats(layer_input):
    widened = layer_input.astype(jnp.float32)
    center = widened - jnp.mean(widened, axis=-1, keepdims=True)
    inv_std = lax.rsqrt(jnp.mean(center * center, axis=-1, keepdims=True) + 1e-06)
    return (center * inv_std, inv_std)


def norm_back(grad_norm, normed, inv_std):
    return inv_std * (
        grad_norm
        - jnp.mean(grad_norm, axis=-1, keepdims=True)
        - normed * jnp.mean(grad_norm * normed, axis=-1, keepdims=True)
    )


def dot(a, b, contract):
    return lax.dot_general(
        a, b, ((contract[:1], contract[1:]), ((), ())), preferred_element_type=jnp.float32
    )


def shift(block, distance):
    count = lax.axis_size("seq")
    route = [(i, i + distance) for i in range(count) if 0 <= i + distance < count]
    return send(block, route)


def spread(target, row, block):
    rows = slice(row, row + block.shape[0])
    used = 2 * HD
    target[rows, :used] = block
    target[rows, used:] = jnp.zeros((block.shape[0], LANES - used), block.dtype)


def spread_queries(source, target):
    tokens, width = source.shape
    for pair in range(width // (2 * HD)):
        spread(target, pair * tokens, source[:, 2 * HD * pair : 2 * HD * (pair + 1)])


def spread_keys(own, before, after, side, target):
    tokens, width = own.shape
    halo = before.shape[1]
    for pair in range(width // (2 * HD)):
        cols = slice(2 * HD * pair, 2 * HD * (pair + 1))
        row = pair * (tokens + 2 * halo)
        spread(target, row, before[side, :, cols])
        spread(target, row + halo, own[:, cols])
        spread(target, row + halo + tokens, after[side, :, cols])


def split_heads(block, first):
    zero = jnp.zeros_like(block)
    return jnp.concatenate(
        [jnp.where(first, block, zero), jnp.where(first, zero, block)], axis=0
    )


def probabilities(ids, start, image, keys, queries):
    scores = dot(keys, queries, (1, 1)) * (float(HD) ** (-0.5) * math.log2(math.e))
    exponent = jnp.concatenate(
        [
            jnp.where(ids[start + j] == image, jnp.exp2(scores[j * TILE : (j + 1) * TILE]), 0.0)
            for j in range(MOST)
        ],
        axis=0,
    )
    return exponent / jnp.sum(exponent, axis=0, keepdims=True)


def over_tiles(tokens, halo, width, step):
    span = tokens + 2 * halo

    def pair_step(pair, carry):
        for i in range(tokens // TILE):
            rows = pl.ds(pl.multiple_of(pair * tokens + i * TILE, TILE), TILE)
            step(i, rows, pair * span)
        return carry

    lax.fori_loop(0, width // (2 * HD), pair_step, 0)


def forward_kernel(ids, starts, q_ref, k_ref, v_ref, before, after, att_ref, qs, ks, vs, at):
    low = jnp.bfloat16
    tokens, width = q_ref.shape
    halo = before.shape[1]
    first = lax.broadcasted_iota(jnp.int32, (1, LANES), 1) < HD
    spread_queries(q_ref, qs)
    spread_keys(k_ref, before, after, 0, ks)
    spread_keys(v_ref, before, after, 1, vs)

    def step(i, rows, base):
        start = starts[i]
        window = pl.ds(pl.multiple_of(base + start * TILE, TILE), MOST * TILE)
        queries = split_heads(qs[rows, :], first)
        prob = probabilities(ids, start, ids[i + halo // TILE], ks[window, :], queries)
        out = dot(prob.astype(low), vs[window, :], (0, 0))
        at[rows, :] = jnp.where(first, out[:TILE], out[TILE:]).astype(low)

    over_tiles(tokens, halo, width, step)
    for pair in range(width // (2 * HD)):
        cols = slice(2 * HD * pair, 2 * HD * (pair + 1))
        att_ref[:, cols] = at[pair * tokens : (pair + 1) * tokens, : 2 * HD]


def backward_kernel(
    ids, starts, q_ref, u_ref, k_ref, v_ref, before, after,
    dq_ref, dk_ref, dv_ref, dbefore, dafter,
    qs, us, ks, vs, gk, gv, dqs,
):
    low = jnp.bfloat16
    tokens, width = q_ref.shape
    halo = before.shape[1]
    span = tokens + 2 * halo
    factor = float(HD) ** (-0.5)
    first = lax.broadcasted_iota(jnp.int32, (1, LANES), 1) < HD
    spread_queries(q_ref, qs)
    spread_queries(u_ref, us)
    spread_keys(k_ref, before, after, 0, ks)
    spread_keys(v_ref, before, after, 1, vs)
    gk[...] = jnp.zeros(gk.shape, jnp.float32)
    gv[...] = jnp.zeros(gv.shape, jnp.float32)

    def step(i, rows, base):
        start = starts[i]
        window = pl.ds(pl.multiple_of(base + start * TILE, TILE), MOST * TILE)
        queries = split_heads(qs[rows, :], first)
        upstream = split_heads(us[rows, :], first)
        keys = ks[window, :]
        prob = probabilities(ids, start, ids[i + halo // TILE], keys, queries)
        dprob = dot(vs[window, :], upstream, (1, 1))
        prob_low = prob.astype(low)
        delta = jnp.sum(prob_low.astype(jnp.float32) * dprob, axis=0, keepdims=True)
        dscore = (prob * (dprob - delta) * factor).astype(low)
        out = dot(dscore, keys, (0, 0))
        dqs[rows, :] = jnp.where(first, out[:TILE], out[TILE:]).astype(low)
        gv[window, :] += dot(prob_low, upstream, (1, 0))
        gk[window, :] += dot(dscore, queries, (1, 0))

    over_tiles(tokens, halo, width, step)
    for pair in range(width // (2 * HD)):
        cols = slice(2 * HD * pair, 2 * HD * (pair + 1))
        dq_ref[:, cols] = dqs[pair * tokens : (pair + 1) * tokens, : 2 * HD]
        row = pair * span
        for source, own, side in ((gk, dk_ref, 0), (gv, dv_ref, 1)):
            dbefore[side, :, cols] = source[row : row + halo, : 2 * HD].astype(low)
            own[:, cols] = source[row + halo : row + halo + tokens, : 2 * HD].astype(low)
            dafter[side, :, cols] = source[row + halo + tokens : row + span, : 2 * HD].astype(low)


def attend(kernel, tables, arrays, results, scratch):
    low = jnp.bfloat16
    return pl.pallas_call(
        kernel,
        in_specs=[pl.BlockSpec(memory_space=pltpu.SMEM)] * len(tables)
        + [pl.BlockSpec(memory_space=pltpu.VMEM)] * len(arrays),
        out_specs=[pl.BlockSpec(memory_space=pltpu.VMEM)] * len(results),
        out_shape=[jax.ShapeDtypeStruct(x.shape, low) for x in results],
        scratch_shapes=[pltpu.VMEM((rows, LANES), dtype) for rows, dtype in scratch],
    )(*tables, *arrays)


def per_device(layer_input, grad_output, tile_image, qkv_weight, out_weight):
    low, wide = jnp.bfloat16, jnp.float32
    tokens = layer_input.shape[0]
    own_rows, width = out_weight.shape
    weights = gather_rows(
        {"k": qkv_weight[:, 1], "v": qkv_weight[:, 2], "q": qkv_weight[:, 0], "o": out_weight}
    )
    half = weights["k"][0].shape[0]
    order = order_matrix(own_rows)
    normed, inv_std = layer_stats(dot(layer_input, order, (1, 0)).astype(low))
    normed_low = normed.astype(low)
    grad_out = dot(grad_output, order, (1, 0)).astype(low)

    def project(rows, name):
        near, far = weights[name]
        return (dot(rows[:, :half], near, (1, 0)) + dot(rows[:, half:], far, (1, 0))).astype(low)

    key, value, query = [project(normed_low, name) for name in "kvq"]
    edge = tokens - HALO
    before = shift(jnp.stack([key[edge:], value[edge:]]), 1)
    after = shift(jnp.stack([key[:HALO], value[:HALO]]), -1)
    tiles_dev = tokens // TILE
    reach = HALO // TILE
    base = lax.axis_index("seq") * tiles_dev
    padded_ids = jnp.pad(tile_image, (reach, reach), constant_values=-1)
    ids = lax.dynamic_slice_in_dim(padded_ids, base, tiles_dev + 2 * reach, 0)
    starts = jnp.clip(
        ids[reach : reach + tiles_dev] - base + reach, 0, tiles_dev + 2 * reach - MOST
    )
    pairs = width // (2 * HD)
    span = tokens + 2 * HALO
    query_rows, key_rows = (pairs * tokens, low), (pairs * span, low)
    sum_rows = (pairs * span, wide)
    (attended,) = attend(
        forward_kernel, (ids, starts), (query, key, value, before, after), (query,),
        (query_rows, key_rows, key_rows, query_rows),
    )
    _, far_o = scatter_far(grad_out, attended)
    _, across_o = scatter_near(grad_out, attended, far_o)
    upstream = project(grad_out, "o")
    dquery, dkey, dvalue, dbefore, dafter = attend(
        backward_kernel, (ids, starts),
        (query, upstream, key, value, before, after),
        (query, key, value, before, after),
        (query_rows, query_rows, key_rows, key_rows, sum_rows, sum_rows, query_rows),
    )
    from_next = shift(dbefore, -1)
    from_prev = shift(dafter, 1)
    _, far_q = scatter_far(normed_low, dquery)
    near_q, across_q = scatter_near(normed_low, dquery, far_q)
    from_next, from_prev, _ = lax.optimization_barrier((from_next, from_prev, near_q))
    own = []
    for side, grad in enumerate((dkey, dvalue)):
        grad = grad.astype(wide)
        grad = grad + jnp.pad(from_prev[side].astype(wide), ((0, edge), (0, 0)))
        grad = grad + jnp.pad(from_next[side].astype(wide), ((edge, 0), (0, 0)))
        own.append(grad.astype(low))
    dkey, dvalue = own
    block_v, far_v = scatter_far(normed_low, dvalue)
    block_k, far_k = scatter_far(normed_low, dkey)
    *grads, _, _ = lax.optimization_barrier((dquery, dkey, dvalue, block_v, block_k))
    grad_norm = [
        sum(dot(grad, weights[name][side], (1, 1)) for name, grad in zip("qkv", grads))
        for side in range(2)
    ]
    _, blocks_o = scatter_line(grad_out, attended, far_o, across_o)
    _, across_v = scatter_near(normed_low, dvalue, far_v)
    _, blocks_q = scatter_line(normed_low, dquery, far_q, across_q)
    _, across_k = scatter_near(normed_low, dkey, far_k)
    _, blocks_v = scatter_line(normed_low, dvalue, far_v, across_v)
    line_k, blocks_k = scatter_line(normed_low, dkey, far_k, across_k)
    blocks_o, blocks_q, blocks_v, _ = lax.optimization_barrier(
        (blocks_o, blocks_q, blocks_v, line_k)
    )

    def total_of(blocks):
        return sum(block.astype(wide) for block in blocks)

    out_grad = total_of(blocks_o)
    qkv_grad = jnp.stack([total_of(blocks) for blocks in (blocks_q, blocks_k, blocks_v)], axis=1)
    parts = lax.axis_size("tp")
    if parts == 2:
        total = []
        for ours in grad_norm:
            ours = ours.astype(low)
            theirs = send(ours, [(0, 1), (1, 0)], "tp")
            theirs, _ = lax.optimization_barrier((theirs, line_k))
            total.append(ours.astype(wide) + theirs.astype(wide))
        total = jnp.concatenate(total, axis=1)
        grad_input = norm_back(total, normed, inv_std).astype(low)
    else:
        share = tokens // parts
        first_row = lax.axis_index("tp") * share
        total = jnp.concatenate(grad_norm, axis=1)
        total = lax.psum_scatter(total, "tp", scatter_dimension=0, tiled=True)
        rows = lax.dynamic_slice_in_dim(normed, first_row, share, 0)
        scales = lax.dynamic_slice_in_dim(inv_std, first_row, share, 0)
        piece = norm_back(total, rows, scales).astype(low)
        grad_input = lax.all_gather(piece, "tp", axis=0, tiled=True)
    grad_input = dot(grad_input, order, (1, 1)).astype(low)
    return (grad_input, qkv_grad, out_grad)


def solution(mesh):
    placed = (P("seq", None), P("seq", None), P(), P("seq", None, "tp"), P("seq", "tp"))
    return jax.shard_map(
        per_device,
        mesh=mesh,
        in_specs=placed,
        out_specs=(P("seq", None), P("seq", None, "tp"), P("seq", "tp")),
        check_vma=False,
    )
```

```python
import math

import jax
import jax.numpy as jnp
from jax import lax
from jax.experimental import pallas as pl
from jax.experimental.pallas import tpu as pltpu
from jax.sharding import PartitionSpec as P


HD = 112
TILE = 128
MOST = 4
HALO = 256
LANES = 256


def rings(count):
    lines = count // 4
    core = [(s, s ^ 1) for s in range(count)]
    pair = [(s, s ^ 2) for s in range(count)]

    def turn(k):
        return [(s, (s - 4 * k) % count) for s in range(count)]

    return lines, core, pair, turn


def send(block, route, axis="seq"):
    return lax.ppermute(block, axis, route)


def gather_rows(shards):
    lines, core, pair, turn = rings(lax.axis_size("seq"))
    gathered = {}
    blocks = []
    for name, shard in shards.items():
        if blocks:
            shard, *blocks = lax.optimization_barrier((shard, *blocks))
        blocks = [send(shard, turn(k)) for k in range(1, lines)]
        line = jnp.concatenate([shard, *blocks], axis=0)
        across = send(line, pair)
        half = jnp.concatenate([line, across], axis=0)
        gathered[name] = (half, send(half, core))
    return gathered


def scatter_far(rows_side, cols_side):
    _, core, _, _ = rings(lax.axis_size("seq"))
    half = rows_side.shape[1] // 2
    block = dot(rows_side[:, half:], cols_side, (0, 0)).astype(jnp.bfloat16)
    return block, send(block, core)


def scatter_near(rows_side, cols_side, far):
    _, _, pair, _ = rings(lax.axis_size("seq"))
    half = far.shape[0]
    quarter = half // 2
    near = dot(rows_side[:, quarter:half], cols_side, (0, 0)) + far[quarter:].astype(jnp.float32)
    near = near.astype(jnp.bfloat16)
    return near, send(near, pair)


def scatter_line(rows_side, cols_side, far, across):
    lines, _, _, turn = rings(lax.axis_size("seq"))
    low, wide = jnp.bfloat16, jnp.float32
    quarter = across.shape[0]
    rows = quarter // lines
    far, across, cols_side = lax.optimization_barrier((far, across, cols_side))
    line = dot(rows_side[:, :quarter], cols_side, (0, 0)) + far[:quarter].astype(wide)
    line = (line + across.astype(wide)).astype(low)
    blocks = [line[:rows]]
    for k in range(1, lines):
        piece = line[rows * k : rows * (k + 1)]
        blocks.append(send(piece, turn(lines - k)))
    return line, blocks


def order_matrix(rows):
    lines = lax.axis_size("seq") // 4
    me = lax.axis_index("seq")
    line, pair, core = me // 4, (me // 2) % 2, me % 2
    width = 4 * lines * rows
    place = lax.broadcasted_iota(jnp.int32, (width, width), 1)
    at = place // rows
    source = (
        ((line + at % lines) % lines) * 4
        + (pair ^ ((at // lines) % 2)) * 2
        + (core ^ (at // (2 * lines)))
    )
    wanted = source * rows + place % rows
    have = lax.broadcasted_iota(jnp.int32, (width, width), 0)
    return (have == wanted).astype(jnp.bfloat16)


def layer_stats(layer_input):
    widened = layer_input.astype(jnp.float32)
    center = widened - jnp.mean(widened, axis=-1, keepdims=True)
    inv_std = lax.rsqrt(jnp.mean(center * center, axis=-1, keepdims=True) + 1e-06)
    return (center * inv_std, inv_std)


def norm_back(grad_norm, normed, inv_std):
    return inv_std * (
        grad_norm
        - jnp.mean(grad_norm, axis=-1, keepdims=True)
        - normed * jnp.mean(grad_norm * normed, axis=-1, keepdims=True)
    )


def dot(a, b, contract):
    return lax.dot_general(
        a, b, ((contract[:1], contract[1:]), ((), ())), preferred_element_type=jnp.float32
    )


def shift(block, distance):
    count = lax.axis_size("seq")
    route = [(i, i + distance) for i in range(count) if 0 <= i + distance < count]
    return send(block, route)


def spread(target, row, block):
    rows = slice(row, row + block.shape[0])
    used = 2 * HD
    target[rows, :used] = block
    target[rows, used:] = jnp.zeros((block.shape[0], LANES - used), block.dtype)


def spread_rows(source, target):
    tokens, width = source.shape
    for pair in range(width // (2 * HD)):
        spread(target, pair * tokens, source[:, 2 * HD * pair : 2 * HD * (pair + 1)])


def split_heads(block, first):
    zero = jnp.zeros_like(block)
    return jnp.concatenate(
        [jnp.where(first, block, zero), jnp.where(first, zero, block)], axis=0
    )


def probabilities(ids, start, image, keys, queries):
    scores = dot(keys, queries, (1, 1)) * (float(HD) ** (-0.5) * math.log2(math.e))
    exponent = jnp.concatenate(
        [
            jnp.where(ids[start + j] == image, jnp.exp2(scores[j * TILE : (j + 1) * TILE]), 0.0)
            for j in range(MOST)
        ],
        axis=0,
    )
    return exponent * (1.0 / jnp.sum(exponent, axis=0, keepdims=True))


def over_tiles(tokens, halo, width, step):
    span = tokens + 2 * halo

    def pair_step(pair, carry):
        for i in range(tokens // TILE):
            rows = pl.ds(pl.multiple_of(pair * tokens + i * TILE, TILE), TILE)
            step(i, rows, pair * span)
        return carry

    lax.fori_loop(0, width // (2 * HD), pair_step, 0)


def forward_kernel(ids, starts, q_ref, k_ref, v_ref, att_ref, qs, ks, vs, at):
    low = jnp.bfloat16
    tokens, width = q_ref.shape
    halo = (k_ref.shape[0] - tokens) // 2
    first = lax.broadcasted_iota(jnp.int32, (1, LANES), 1) < HD
    spread_rows(q_ref, qs)
    spread_rows(k_ref, ks)
    spread_rows(v_ref, vs)

    def step(i, rows, base):
        start = starts[i]
        window = pl.ds(pl.multiple_of(base + start * TILE, TILE), MOST * TILE)
        queries = split_heads(qs[rows, :], first)
        prob = probabilities(ids, start, ids[i + halo // TILE], ks[window, :], queries)
        out = dot(prob.astype(low), vs[window, :], (0, 0))
        at[rows, :] = jnp.where(first, out[:TILE], out[TILE:]).astype(low)

    over_tiles(tokens, halo, width, step)
    for pair in range(width // (2 * HD)):
        cols = slice(2 * HD * pair, 2 * HD * (pair + 1))
        att_ref[:, cols] = at[pair * tokens : (pair + 1) * tokens, : 2 * HD]


def backward_kernel(
    ids, starts, q_ref, u_ref, k_ref, v_ref,
    dq_ref, dk_ref, dv_ref, dbefore, dafter,
    qs, us, ks, vs, gk, gv, dqs,
):
    low = jnp.bfloat16
    tokens, width = q_ref.shape
    span = k_ref.shape[0]
    halo = (span - tokens) // 2
    factor = float(HD) ** (-0.5)
    first = lax.broadcasted_iota(jnp.int32, (1, LANES), 1) < HD
    spread_rows(q_ref, qs)
    spread_rows(u_ref, us)
    spread_rows(k_ref, ks)
    spread_rows(v_ref, vs)
    gk[...] = jnp.zeros(gk.shape, jnp.float32)
    gv[...] = jnp.zeros(gv.shape, jnp.float32)

    def step(i, rows, base):
        start = starts[i]
        window = pl.ds(pl.multiple_of(base + start * TILE, TILE), MOST * TILE)
        queries = split_heads(qs[rows, :], first)
        upstream = split_heads(us[rows, :], first)
        keys = ks[window, :]
        prob = probabilities(ids, start, ids[i + halo // TILE], keys, queries)
        dprob = dot(vs[window, :], upstream, (1, 1))
        prob_low = prob.astype(low)
        delta = jnp.sum(prob_low.astype(jnp.float32) * dprob, axis=0, keepdims=True)
        dscore = (prob * (dprob - delta) * factor).astype(low)
        out = dot(dscore, keys, (0, 0))
        dqs[rows, :] = jnp.where(first, out[:TILE], out[TILE:]).astype(low)
        gv[window, :] += dot(prob_low, upstream, (1, 0))
        gk[window, :] += dot(dscore, queries, (1, 0))

    over_tiles(tokens, halo, width, step)
    for pair in range(width // (2 * HD)):
        cols = slice(2 * HD * pair, 2 * HD * (pair + 1))
        dq_ref[:, cols] = dqs[pair * tokens : (pair + 1) * tokens, : 2 * HD]
        row = pair * span
        for source, own, side in ((gk, dk_ref, 0), (gv, dv_ref, 1)):
            block = source[row : row + span, : 2 * HD].astype(low)
            own[:, cols] = block
            dbefore[side, :, cols] = block[:halo]
            dafter[side, :, cols] = block[halo + tokens :]


def attend(kernel, tables, arrays, results, scratch):
    low = jnp.bfloat16
    return pl.pallas_call(
        kernel,
        in_specs=[pl.BlockSpec(memory_space=pltpu.SMEM)] * len(tables)
        + [pl.BlockSpec(memory_space=pltpu.VMEM)] * len(arrays),
        out_specs=[pl.BlockSpec(memory_space=pltpu.VMEM)] * len(results),
        out_shape=[jax.ShapeDtypeStruct(shape, low) for shape in results],
        scratch_shapes=[pltpu.VMEM((rows, LANES), dtype) for rows, dtype in scratch],
    )(*tables, *arrays)


def per_device(layer_input, grad_output, tile_image, qkv_weight, out_weight):
    low, wide = jnp.bfloat16, jnp.float32
    tokens = layer_input.shape[0]
    own_rows, width = out_weight.shape
    weights = gather_rows(
        {"k": qkv_weight[:, 1], "v": qkv_weight[:, 2], "q": qkv_weight[:, 0], "o": out_weight}
    )
    half = weights["k"][0].shape[0]
    order = order_matrix(own_rows)
    edge = tokens - HALO
    before = shift(layer_input[edge:], 1)
    after = shift(layer_input[:HALO], -1)
    inputs = jnp.concatenate([before, layer_input, after], axis=0)
    normed, inv_std = layer_stats(dot(inputs, order, (1, 0)).astype(low))
    normed_wide = normed.astype(low)
    normed, inv_std = normed[HALO : HALO + tokens], inv_std[HALO : HALO + tokens]
    normed_low = normed_wide[HALO : HALO + tokens]
    grad_out = dot(grad_output, order, (1, 0)).astype(low)

    def project(rows, name):
        near, far = weights[name]
        out = dot(rows[:, :half], near, (1, 0)) + dot(rows[:, half:], far, (1, 0))
        return out.astype(low)

    key, value = project(normed_wide, "k"), project(normed_wide, "v")
    query = project(normed_low, "q")
    tiles_dev = tokens // TILE
    reach = HALO // TILE
    base = lax.axis_index("seq") * tiles_dev
    padded_ids = jnp.pad(tile_image, (reach, reach), constant_values=-1)
    ids = lax.dynamic_slice_in_dim(padded_ids, base, tiles_dev + 2 * reach, 0)
    starts = jnp.clip(
        ids[reach : reach + tiles_dev] - base + reach, 0, tiles_dev + 2 * reach - MOST
    )
    pairs = width // (2 * HD)
    span = tokens + 2 * HALO
    query_rows, key_rows = (pairs * tokens, low), (pairs * span, low)
    sum_rows = (pairs * span, wide)
    (attended,) = attend(
        forward_kernel, (ids, starts), (query, key, value), (query.shape,),
        (query_rows, key_rows, key_rows, query_rows),
    )
    _, far_o = scatter_far(grad_out, attended)
    _, across_o = scatter_near(grad_out, attended, far_o)
    upstream = project(grad_out, "o")
    halo_shape = (2, HALO, width)
    dquery, dkey, dvalue, dbefore, dafter = attend(
        backward_kernel, (ids, starts), (query, upstream, key, value),
        (query.shape, key.shape, value.shape, halo_shape, halo_shape),
        (query_rows, query_rows, key_rows, key_rows, sum_rows, sum_rows, query_rows),
    )
    _, far_q = scatter_far(normed_low, dquery)
    _, across_q = scatter_near(normed_low, dquery, far_q)
    from_next = shift(dbefore, -1)
    from_prev = shift(dafter, 1)
    block_v, far_v = scatter_far(normed_wide, dvalue)
    block_k, far_k = scatter_far(normed_wide, dkey)
    from_next, from_prev, dq, _, _ = lax.optimization_barrier(
        (from_next, from_prev, dquery, block_v, block_k)
    )
    grads = [dq]
    for side, grad in enumerate((dkey, dvalue)):
        grad = grad[HALO : HALO + tokens].astype(wide)
        grad = grad + jnp.pad(from_prev[side].astype(wide), ((0, edge), (0, 0)))
        grad = grad + jnp.pad(from_next[side].astype(wide), ((edge, 0), (0, 0)))
        grads.append(grad.astype(low))
    grad_norm = [
        sum(dot(grad, weights[name][side], (1, 1)) for name, grad in zip("qkv", grads))
        for side in range(2)
    ]
    _, blocks_o = scatter_line(grad_out, attended, far_o, across_o)
    _, across_v = scatter_near(normed_wide, dvalue, far_v)
    _, blocks_q = scatter_line(normed_low, dquery, far_q, across_q)
    _, across_k = scatter_near(normed_wide, dkey, far_k)
    _, blocks_v = scatter_line(normed_wide, dvalue, far_v, across_v)
    line_k, blocks_k = scatter_line(normed_wide, dkey, far_k, across_k)
    blocks_o, blocks_q, blocks_v, _ = lax.optimization_barrier(
        (blocks_o, blocks_q, blocks_v, line_k)
    )

    def total_of(blocks):
        return sum(block.astype(wide) for block in blocks)

    out_grad = total_of(blocks_o)
    qkv_grad = jnp.stack([total_of(blocks) for blocks in (blocks_q, blocks_k, blocks_v)], axis=1)
    parts = lax.axis_size("tp")
    if parts == 2:
        total = []
        for ours in grad_norm:
            ours = ours.astype(low)
            theirs = send(ours, [(0, 1), (1, 0)], "tp")
            theirs, _ = lax.optimization_barrier((theirs, line_k))
            total.append(ours.astype(wide) + theirs.astype(wide))
        total = jnp.concatenate(total, axis=1)
        grad_input = norm_back(total, normed, inv_std).astype(low)
    else:
        share = tokens // parts
        first_row = lax.axis_index("tp") * share
        total = jnp.concatenate(grad_norm, axis=1)
        total = lax.psum_scatter(total, "tp", scatter_dimension=0, tiled=True)
        rows = lax.dynamic_slice_in_dim(normed, first_row, share, 0)
        scales = lax.dynamic_slice_in_dim(inv_std, first_row, share, 0)
        piece = norm_back(total, rows, scales).astype(low)
        grad_input = lax.all_gather(piece, "tp", axis=0, tiled=True)
    grad_input = dot(grad_input, order, (1, 1)).astype(low)
    return (grad_input, qkv_grad, out_grad)


def solution(mesh):
    placed = (P("seq", None), P("seq", None), P(), P("seq", None, "tp"), P("seq", "tp"))
    return jax.shard_map(
        per_device,
        mesh=mesh,
        in_specs=placed,
        out_specs=(P("seq", None), P("seq", None, "tp"), P("seq", "tp")),
        check_vma=False,
    )
```

```python
import math

import jax
import jax.numpy as jnp
from jax import lax
from jax.experimental import pallas as pl
from jax.experimental.pallas import tpu as pltpu
from jax.sharding import PartitionSpec as P


HD = 112
TILE = 128
MOST = 4
HALO = 256
LANES = 256


def rings(count):
    lines = count // 4
    core = [(s, s ^ 1) for s in range(count)]
    pair = [(s, s ^ 2) for s in range(count)]

    def turn(k):
        return [(s, (s - 4 * k) % count) for s in range(count)]

    return lines, core, pair, turn


def send(block, route, axis="seq"):
    return lax.ppermute(block, axis, route)


def gather_rows(shards):
    lines, core, pair, turn = rings(lax.axis_size("seq"))
    gathered = {}
    for name, shard in shards.items():
        blocks = [send(shard, turn(k)) for k in range(1, lines)]
        line = jnp.concatenate([shard, *blocks], axis=0)
        across = send(line, pair)
        half = jnp.concatenate([line, across], axis=0)
        gathered[name] = (half, send(half, core))
    return gathered


def scatter_far(rows_side, cols_side):
    _, core, _, _ = rings(lax.axis_size("seq"))
    half = rows_side.shape[1] // 2
    block = dot(rows_side[:, half:], cols_side, (0, 0)).astype(jnp.bfloat16)
    return block, send(block, core)


def scatter_near(rows_side, cols_side, far):
    _, _, pair, _ = rings(lax.axis_size("seq"))
    half = far.shape[0]
    quarter = half // 2
    near = dot(rows_side[:, quarter:half], cols_side, (0, 0))
    near = (near + far[quarter:].astype(jnp.float32)).astype(jnp.bfloat16)
    return near, send(near, pair)


def scatter_line(rows_side, cols_side, far, across):
    lines, _, _, turn = rings(lax.axis_size("seq"))
    low, wide = jnp.bfloat16, jnp.float32
    quarter = across.shape[0]
    rows = quarter // lines
    far, across, cols_side = lax.optimization_barrier((far, across, cols_side))
    line = dot(rows_side[:, :quarter], cols_side, (0, 0)) + far[:quarter].astype(wide)
    line = (line + across.astype(wide)).astype(low)
    blocks = [line[:rows]]
    for k in range(1, lines):
        piece = line[rows * k : rows * (k + 1)]
        blocks.append(send(piece, turn(lines - k)))
    return line, blocks


def order_matrix(rows):
    lines = lax.axis_size("seq") // 4
    me = lax.axis_index("seq")
    line, pair, core = me // 4, (me // 2) % 2, me % 2
    width = 4 * lines * rows
    place = lax.broadcasted_iota(jnp.int32, (width, width), 1)
    at = place // rows
    source = (
        ((line + at % lines) % lines) * 4
        + (pair ^ ((at // lines) % 2)) * 2
        + (core ^ (at // (2 * lines)))
    )
    wanted = source * rows + place % rows
    have = lax.broadcasted_iota(jnp.int32, (width, width), 0)
    return (have == wanted).astype(jnp.bfloat16)


def layer_stats(layer_input):
    widened = layer_input.astype(jnp.float32)
    center = widened - jnp.mean(widened, axis=-1, keepdims=True)
    inv_std = lax.rsqrt(jnp.mean(center * center, axis=-1, keepdims=True) + 1e-06)
    return (center * inv_std, inv_std)


def norm_back(grad_norm, normed, inv_std):
    return inv_std * (
        grad_norm
        - jnp.mean(grad_norm, axis=-1, keepdims=True)
        - normed * jnp.mean(grad_norm * normed, axis=-1, keepdims=True)
    )


def dot(a, b, contract):
    return lax.dot_general(
        a, b, ((contract[:1], contract[1:]), ((), ())), preferred_element_type=jnp.float32
    )


def shift(block, distance):
    count = lax.axis_size("seq")
    route = [(i, i + distance) for i in range(count) if 0 <= i + distance < count]
    return send(block, route)


def spread(target, row, block):
    rows = slice(row, row + block.shape[0])
    used = 2 * HD
    target[rows, :used] = block
    target[rows, used:] = jnp.zeros((block.shape[0], LANES - used), block.dtype)


def spread_rows(source, target):
    tokens, width = source.shape
    for pair in range(width // (2 * HD)):
        spread(target, pair * tokens, source[:, 2 * HD * pair : 2 * HD * (pair + 1)])


def split_heads(block, first):
    zero = jnp.zeros_like(block)
    return jnp.concatenate(
        [jnp.where(first, block, zero), jnp.where(first, zero, block)], axis=0
    )


def probabilities(ids, start, image, keys, queries):
    scores = dot(keys, queries, (1, 1)) * (float(HD) ** (-0.5) * math.log2(math.e))
    exponent = jnp.concatenate(
        [
            jnp.where(ids[start + j] == image, jnp.exp2(scores[j * TILE : (j + 1) * TILE]), 0.0)
            for j in range(MOST)
        ],
        axis=0,
    )
    return exponent * (1.0 / jnp.sum(exponent, axis=0, keepdims=True))


def over_tiles(tokens, halo, width, step):
    span = tokens + 2 * halo

    def pair_step(pair, carry):
        for i in range(tokens // TILE):
            rows = pl.ds(pl.multiple_of(pair * tokens + i * TILE, TILE), TILE)
            step(i, rows, pair * span)
        return carry

    lax.fori_loop(0, width // (2 * HD), pair_step, 0)


def forward_kernel(ids, starts, q_ref, k_ref, v_ref, att_ref, qs, ks, vs, at):
    low = jnp.bfloat16
    tokens, width = q_ref.shape
    halo = (k_ref.shape[0] - tokens) // 2
    first = lax.broadcasted_iota(jnp.int32, (1, LANES), 1) < HD
    spread_rows(q_ref, qs)
    spread_rows(k_ref, ks)
    spread_rows(v_ref, vs)

    def step(i, rows, base):
        start = starts[i]
        window = pl.ds(pl.multiple_of(base + start * TILE, TILE), MOST * TILE)
        queries = split_heads(qs[rows, :], first)
        prob = probabilities(ids, start, ids[i + halo // TILE], ks[window, :], queries)
        out = dot(prob.astype(low), vs[window, :], (0, 0))
        at[rows, :] = jnp.where(first, out[:TILE], out[TILE:]).astype(low)

    over_tiles(tokens, halo, width, step)
    for pair in range(width // (2 * HD)):
        cols = slice(2 * HD * pair, 2 * HD * (pair + 1))
        att_ref[:, cols] = at[pair * tokens : (pair + 1) * tokens, : 2 * HD]


def backward_kernel(
    ids, starts, q_ref, u_ref, k_ref, v_ref,
    dq_ref, dk_ref, dv_ref, dbefore, dafter,
    qs, us, ks, vs, gk, gv, dqs,
):
    low = jnp.bfloat16
    tokens, width = q_ref.shape
    span = k_ref.shape[0]
    halo = (span - tokens) // 2
    factor = float(HD) ** (-0.5)
    first = lax.broadcasted_iota(jnp.int32, (1, LANES), 1) < HD
    spread_rows(q_ref, qs)
    spread_rows(u_ref, us)
    spread_rows(k_ref, ks)
    spread_rows(v_ref, vs)
    gk[...] = jnp.zeros(gk.shape, jnp.float32)
    gv[...] = jnp.zeros(gv.shape, jnp.float32)

    def step(i, rows, base):
        start = starts[i]
        window = pl.ds(pl.multiple_of(base + start * TILE, TILE), MOST * TILE)
        queries = split_heads(qs[rows, :], first)
        upstream = split_heads(us[rows, :], first)
        keys = ks[window, :]
        prob = probabilities(ids, start, ids[i + halo // TILE], keys, queries)
        dprob = dot(vs[window, :], upstream, (1, 1))
        prob_low = prob.astype(low)
        delta = jnp.sum(prob_low.astype(jnp.float32) * dprob, axis=0, keepdims=True)
        dscore = (prob * (dprob - delta) * factor).astype(low)
        out = dot(dscore, keys, (0, 0))
        dqs[rows, :] = jnp.where(first, out[:TILE], out[TILE:]).astype(low)
        gv[window, :] += dot(prob_low, upstream, (1, 0))
        gk[window, :] += dot(dscore, queries, (1, 0))

    over_tiles(tokens, halo, width, step)
    for pair in range(width // (2 * HD)):
        cols = slice(2 * HD * pair, 2 * HD * (pair + 1))
        dq_ref[:, cols] = dqs[pair * tokens : (pair + 1) * tokens, : 2 * HD]
        row = pair * span
        for source, own, side in ((gk, dk_ref, 0), (gv, dv_ref, 1)):
            block = source[row : row + span, : 2 * HD].astype(low)
            own[:, cols] = block
            dbefore[side, :, cols] = block[:halo]
            dafter[side, :, cols] = block[halo + tokens :]


def attend(kernel, tables, arrays, results, scratch):
    low = jnp.bfloat16
    return pl.pallas_call(
        kernel,
        in_specs=[pl.BlockSpec(memory_space=pltpu.SMEM)] * len(tables)
        + [pl.BlockSpec(memory_space=pltpu.VMEM)] * len(arrays),
        out_specs=[pl.BlockSpec(memory_space=pltpu.VMEM)] * len(results),
        out_shape=[jax.ShapeDtypeStruct(shape, low) for shape in results],
        scratch_shapes=[pltpu.VMEM((rows, LANES), dtype) for rows, dtype in scratch],
    )(*tables, *arrays)


def per_device(layer_input, grad_output, tile_image, qkv_weight, out_weight):
    low, wide = jnp.bfloat16, jnp.float32
    tokens = layer_input.shape[0]
    own_rows, width = out_weight.shape
    weights = gather_rows(
        {"k": qkv_weight[:, 1], "v": qkv_weight[:, 2], "q": qkv_weight[:, 0], "o": out_weight}
    )
    half = weights["k"][0].shape[0]
    order = order_matrix(own_rows)
    edge = tokens - HALO
    before = shift(layer_input[edge:], 1)
    after = shift(layer_input[:HALO], -1)
    inputs = jnp.concatenate([before, layer_input, after], axis=0)
    normed, inv_std = layer_stats(dot(inputs, order, (1, 0)).astype(low))
    normed_wide = normed.astype(low)
    normed, inv_std = normed[HALO : HALO + tokens], inv_std[HALO : HALO + tokens]
    normed_low = normed_wide[HALO : HALO + tokens]
    grad_out = dot(grad_output, order, (1, 0)).astype(low)

    def project(rows, name):
        near, far = weights[name]
        out = dot(rows[:, :half], near, (1, 0)) + dot(rows[:, half:], far, (1, 0))
        return out.astype(low)

    key, value = project(normed_wide, "k"), project(normed_wide, "v")
    query = project(normed_low, "q")
    tiles_dev = tokens // TILE
    reach = HALO // TILE
    base = lax.axis_index("seq") * tiles_dev
    padded_ids = jnp.pad(tile_image, (reach, reach), constant_values=-1)
    ids = lax.dynamic_slice_in_dim(padded_ids, base, tiles_dev + 2 * reach, 0)
    starts = jnp.clip(
        ids[reach : reach + tiles_dev] - base + reach, 0, tiles_dev + 2 * reach - MOST
    )
    pairs = width // (2 * HD)
    span = tokens + 2 * HALO
    query_rows, key_rows = (pairs * tokens, low), (pairs * span, low)
    sum_rows = (pairs * span, wide)
    (attended,) = attend(
        forward_kernel, (ids, starts), (query, key, value), (query.shape,),
        (query_rows, key_rows, key_rows, query_rows),
    )
    _, far_o = scatter_far(grad_out, attended)
    _, across_o = scatter_near(grad_out, attended, far_o)
    upstream = project(grad_out, "o")
    halo_shape = (2, HALO, width)
    dquery, dkey, dvalue, dbefore, dafter = attend(
        backward_kernel, (ids, starts), (query, upstream, key, value),
        (query.shape, key.shape, value.shape, halo_shape, halo_shape),
        (query_rows, query_rows, key_rows, key_rows, sum_rows, sum_rows, query_rows),
    )
    _, far_q = scatter_far(normed_low, dquery)
    _, across_q = scatter_near(normed_low, dquery, far_q)
    from_next = shift(dbefore, -1)
    from_prev = shift(dafter, 1)
    block_v, far_v = scatter_far(normed_wide, dvalue)
    block_k, far_k = scatter_far(normed_wide, dkey)
    from_next, from_prev, dq, _, _ = lax.optimization_barrier(
        (from_next, from_prev, dquery, block_v, block_k)
    )
    grads = [dq]
    for side, grad in enumerate((dkey, dvalue)):
        grad = grad[HALO : HALO + tokens].astype(wide)
        grad = grad + jnp.pad(from_prev[side].astype(wide), ((0, edge), (0, 0)))
        grad = grad + jnp.pad(from_next[side].astype(wide), ((edge, 0), (0, 0)))
        grads.append(grad.astype(low))
    grad_norm = [
        sum(dot(grad, weights[name][side], (1, 1)) for name, grad in zip("qkv", grads))
        for side in range(2)
    ]
    _, blocks_o = scatter_line(grad_out, attended, far_o, across_o)
    _, across_v = scatter_near(normed_wide, dvalue, far_v)
    _, blocks_q = scatter_line(normed_low, dquery, far_q, across_q)
    _, across_k = scatter_near(normed_wide, dkey, far_k)
    _, blocks_v = scatter_line(normed_wide, dvalue, far_v, across_v)
    line_k, blocks_k = scatter_line(normed_wide, dkey, far_k, across_k)
    blocks_o, blocks_q, blocks_v, blocks_k = lax.optimization_barrier(
        (blocks_o, blocks_q, blocks_v, blocks_k)
    )

    def total_of(blocks):
        return sum(block.astype(wide) for block in blocks)

    out_grad = total_of(blocks_o)
    qkv_grad = jnp.stack([total_of(blocks) for blocks in (blocks_q, blocks_k, blocks_v)], axis=1)
    parts = lax.axis_size("tp")
    if parts == 2:
        total = []
        for ours in grad_norm:
            ours = ours.astype(low)
            theirs = send(ours, [(0, 1), (1, 0)], "tp")
            theirs, _ = lax.optimization_barrier((theirs, line_k))
            total.append(ours.astype(wide) + theirs.astype(wide))
        total = jnp.concatenate(total, axis=1)
        grad_input = norm_back(total, normed, inv_std).astype(low)
    else:
        share = tokens // parts
        first_row = lax.axis_index("tp") * share
        total = jnp.concatenate(grad_norm, axis=1)
        total = lax.psum_scatter(total, "tp", scatter_dimension=0, tiled=True)
        rows = lax.dynamic_slice_in_dim(normed, first_row, share, 0)
        scales = lax.dynamic_slice_in_dim(inv_std, first_row, share, 0)
        piece = norm_back(total, rows, scales).astype(low)
        grad_input = lax.all_gather(piece, "tp", axis=0, tiled=True)
    grad_input = dot(grad_input, order, (1, 1)).astype(low)
    return (grad_input, qkv_grad, out_grad)


def solution(mesh):
    placed = (P("seq", None), P("seq", None), P(), P("seq", None, "tp"), P("seq", "tp"))
    return jax.shard_map(
        per_device,
        mesh=mesh,
        in_specs=placed,
        out_specs=(P("seq", None), P("seq", None, "tp"), P("seq", "tp")),
        check_vma=False,
    )
```

```python
import math

import jax
import jax.numpy as jnp
from jax import lax
from jax.experimental import pallas as pl
from jax.experimental.pallas import tpu as pltpu
from jax.sharding import PartitionSpec as P


HD = 112
TILE = 128
MOST = 4
HALO = 256
LANES = 256


def rings(count):
    lines = count // 4
    core = [(s, s ^ 1) for s in range(count)]
    pair = [(s, s ^ 2) for s in range(count)]

    def turn(k):
        return [(s, (s - 4 * k) % count) for s in range(count)]

    return lines, core, pair, turn


def send(block, route, axis="seq"):
    return lax.ppermute(block, axis, route)


def gather_rows(shards):
    lines, core, pair, turn = rings(lax.axis_size("seq"))
    gathered = {}
    ahead = []
    for name, shard in shards.items():
        if ahead:
            shard, *ahead = lax.optimization_barrier((shard, *ahead))
        blocks = {0: shard, lines: shard}
        for k in range(1, lines // 2 + 1):
            blocks[k] = send(blocks[k - 1], turn(1))
            if k < lines - k:
                blocks[lines - k] = send(blocks[lines - k + 1], turn(lines - 1))
        blocks = [blocks[k] for k in range(1, lines)]
        ahead = [blocks[0], blocks[-1]] if gathered else blocks
        line = jnp.concatenate([shard, *blocks], axis=0)
        across = send(line, pair)
        half = jnp.concatenate([line, across], axis=0)
        gathered[name] = (half, send(half, core))
    return gathered


def scatter_far(rows_side, cols_side):
    _, core, _, _ = rings(lax.axis_size("seq"))
    half = rows_side.shape[1] // 2
    block = dot(rows_side[:, half:], cols_side, (0, 0)).astype(jnp.bfloat16)
    return block, send(block, core)


def scatter_near(rows_side, cols_side, far):
    _, _, pair, _ = rings(lax.axis_size("seq"))
    half = far.shape[0]
    quarter = half // 2
    near = dot(rows_side[:, quarter:half], cols_side, (0, 0))
    near = (near + far[quarter:].astype(jnp.float32)).astype(jnp.bfloat16)
    return near, send(near, pair)


def scatter_line(rows_side, cols_side, far, across):
    lines, _, _, turn = rings(lax.axis_size("seq"))
    low, wide = jnp.bfloat16, jnp.float32
    quarter = across.shape[0]
    rows = quarter // lines
    far, across, cols_side = lax.optimization_barrier((far, across, cols_side))
    line = dot(rows_side[:, :quarter], cols_side, (0, 0)) + far[:quarter].astype(wide)
    line = (line + across.astype(wide)).astype(low)
    blocks = [line[:rows]]
    for k in range(1, lines):
        piece = line[rows * k : rows * (k + 1)]
        blocks.append(send(piece, turn(lines - k)))
    return line, blocks


def order_matrix(rows):
    lines = lax.axis_size("seq") // 4
    me = lax.axis_index("seq")
    line, pair, core = me // 4, (me // 2) % 2, me % 2
    width = 4 * lines * rows
    place = lax.broadcasted_iota(jnp.int32, (width, width), 1)
    at = place // rows
    source = (
        ((line + at % lines) % lines) * 4
        + (pair ^ ((at // lines) % 2)) * 2
        + (core ^ (at // (2 * lines)))
    )
    wanted = source * rows + place % rows
    have = lax.broadcasted_iota(jnp.int32, (width, width), 0)
    return (have == wanted).astype(jnp.bfloat16)


def layer_stats(layer_input):
    widened = layer_input.astype(jnp.float32)
    center = widened - jnp.mean(widened, axis=-1, keepdims=True)
    inv_std = lax.rsqrt(jnp.mean(center * center, axis=-1, keepdims=True) + 1e-06)
    return (center * inv_std, inv_std)


def norm_back(grad_norm, normed, inv_std):
    return inv_std * (
        grad_norm
        - jnp.mean(grad_norm, axis=-1, keepdims=True)
        - normed * jnp.mean(grad_norm * normed, axis=-1, keepdims=True)
    )


def dot(a, b, contract):
    return lax.dot_general(
        a, b, ((contract[:1], contract[1:]), ((), ())), preferred_element_type=jnp.float32
    )


def shift(block, distance):
    count = lax.axis_size("seq")
    route = [(i, i + distance) for i in range(count) if 0 <= i + distance < count]
    return send(block, route)


def spread(target, row, block):
    rows = slice(row, row + block.shape[0])
    used = 2 * HD
    target[rows, :used] = block
    target[rows, used:] = jnp.zeros((block.shape[0], LANES - used), block.dtype)


def spread_rows(source, target):
    tokens, width = source.shape
    for pair in range(width // (2 * HD)):
        spread(target, pair * tokens, source[:, 2 * HD * pair : 2 * HD * (pair + 1)])


def split_heads(block, first):
    zero = jnp.zeros_like(block)
    return jnp.concatenate(
        [jnp.where(first, block, zero), jnp.where(first, zero, block)], axis=0
    )


def probabilities(ids, start, image, keys, queries):
    scores = dot(keys, queries, (1, 1)) * (float(HD) ** (-0.5) * math.log2(math.e))
    exponent = jnp.concatenate(
        [
            jnp.where(ids[start + j] == image, jnp.exp2(scores[j * TILE : (j + 1) * TILE]), 0.0)
            for j in range(MOST)
        ],
        axis=0,
    )
    return exponent * (1.0 / jnp.sum(exponent, axis=0, keepdims=True))


def over_tiles(tokens, halo, width, step):
    span = tokens + 2 * halo

    def pair_step(pair, carry):
        for i in range(tokens // TILE):
            rows = pl.ds(pl.multiple_of(pair * tokens + i * TILE, TILE), TILE)
            step(i, rows, pair * span)
        return carry

    lax.fori_loop(0, width // (2 * HD), pair_step, 0)


def forward_kernel(ids, starts, q_ref, k_ref, v_ref, att_ref, qs, ks, vs, at):
    low = jnp.bfloat16
    tokens, width = q_ref.shape
    halo = (k_ref.shape[0] - tokens) // 2
    first = lax.broadcasted_iota(jnp.int32, (1, LANES), 1) < HD
    spread_rows(q_ref, qs)
    spread_rows(k_ref, ks)
    spread_rows(v_ref, vs)

    def step(i, rows, base):
        start = starts[i]
        window = pl.ds(pl.multiple_of(base + start * TILE, TILE), MOST * TILE)
        queries = split_heads(qs[rows, :], first)
        prob = probabilities(ids, start, ids[i + halo // TILE], ks[window, :], queries)
        out = dot(prob.astype(low), vs[window, :], (0, 0))
        at[rows, :] = jnp.where(first, out[:TILE], out[TILE:]).astype(low)

    over_tiles(tokens, halo, width, step)
    for pair in range(width // (2 * HD)):
        cols = slice(2 * HD * pair, 2 * HD * (pair + 1))
        att_ref[:, cols] = at[pair * tokens : (pair + 1) * tokens, : 2 * HD]


def backward_kernel(
    ids, starts, q_ref, u_ref, k_ref, v_ref,
    dq_ref, dk_ref, dv_ref, dbefore, dafter,
    qs, us, ks, vs, gk, gv, dqs,
):
    low = jnp.bfloat16
    tokens, width = q_ref.shape
    span = k_ref.shape[0]
    halo = (span - tokens) // 2
    factor = float(HD) ** (-0.5)
    first = lax.broadcasted_iota(jnp.int32, (1, LANES), 1) < HD
    spread_rows(q_ref, qs)
    spread_rows(u_ref, us)
    spread_rows(k_ref, ks)
    spread_rows(v_ref, vs)
    gk[...] = jnp.zeros(gk.shape, jnp.float32)
    gv[...] = jnp.zeros(gv.shape, jnp.float32)

    def step(i, rows, base):
        start = starts[i]
        window = pl.ds(pl.multiple_of(base + start * TILE, TILE), MOST * TILE)
        queries = split_heads(qs[rows, :], first)
        upstream = split_heads(us[rows, :], first)
        keys = ks[window, :]
        prob = probabilities(ids, start, ids[i + halo // TILE], keys, queries)
        dprob = dot(vs[window, :], upstream, (1, 1))
        prob_low = prob.astype(low)
        delta = jnp.sum(prob_low.astype(jnp.float32) * dprob, axis=0, keepdims=True)
        dscore = (prob * (dprob - delta) * factor).astype(low)
        out = dot(dscore, keys, (0, 0))
        dqs[rows, :] = jnp.where(first, out[:TILE], out[TILE:]).astype(low)
        gv[window, :] += dot(prob_low, upstream, (1, 0))
        gk[window, :] += dot(dscore, queries, (1, 0))

    over_tiles(tokens, halo, width, step)
    for pair in range(width // (2 * HD)):
        cols = slice(2 * HD * pair, 2 * HD * (pair + 1))
        dq_ref[:, cols] = dqs[pair * tokens : (pair + 1) * tokens, : 2 * HD]
        row = pair * span
        for source, own, side in ((gk, dk_ref, 0), (gv, dv_ref, 1)):
            block = source[row : row + span, : 2 * HD].astype(low)
            own[:, cols] = block
            dbefore[side, :, cols] = block[:halo]
            dafter[side, :, cols] = block[halo + tokens :]


def attend(kernel, tables, arrays, results, scratch):
    low = jnp.bfloat16
    return pl.pallas_call(
        kernel,
        in_specs=[pl.BlockSpec(memory_space=pltpu.SMEM)] * len(tables)
        + [pl.BlockSpec(memory_space=pltpu.VMEM)] * len(arrays),
        out_specs=[pl.BlockSpec(memory_space=pltpu.VMEM)] * len(results),
        out_shape=[jax.ShapeDtypeStruct(shape, low) for shape in results],
        scratch_shapes=[pltpu.VMEM((rows, LANES), dtype) for rows, dtype in scratch],
    )(*tables, *arrays)


def per_device(layer_input, grad_output, tile_image, qkv_weight, out_weight):
    low, wide = jnp.bfloat16, jnp.float32
    tokens = layer_input.shape[0]
    own_rows, width = out_weight.shape
    weights = gather_rows(
        {"k": qkv_weight[:, 1], "v": qkv_weight[:, 2], "q": qkv_weight[:, 0], "o": out_weight}
    )
    half = weights["k"][0].shape[0]
    order = order_matrix(own_rows)
    edge = tokens - HALO
    before = shift(layer_input[edge:], 1)
    after = shift(layer_input[:HALO], -1)
    inputs = jnp.concatenate([before, layer_input, after], axis=0)
    normed, inv_std = layer_stats(dot(inputs, order, (1, 0)).astype(low))
    normed_wide = normed.astype(low)
    normed, inv_std = normed[HALO : HALO + tokens], inv_std[HALO : HALO + tokens]
    normed_low = normed_wide[HALO : HALO + tokens]
    grad_out = dot(grad_output, order, (1, 0)).astype(low)

    def project(rows, name):
        near, far = weights[name]
        out = dot(rows[:, :half], near, (1, 0)) + dot(rows[:, half:], far, (1, 0))
        return out.astype(low)

    key, value = project(normed_wide, "k"), project(normed_wide, "v")
    query = project(normed_low, "q")
    tiles_dev = tokens // TILE
    reach = HALO // TILE
    base = lax.axis_index("seq") * tiles_dev
    padded_ids = jnp.pad(tile_image, (reach, reach), constant_values=-1)
    ids = lax.dynamic_slice_in_dim(padded_ids, base, tiles_dev + 2 * reach, 0)
    starts = jnp.clip(
        ids[reach : reach + tiles_dev] - base + reach, 0, tiles_dev + 2 * reach - MOST
    )
    pairs = width // (2 * HD)
    span = tokens + 2 * HALO
    query_rows, key_rows = (pairs * tokens, low), (pairs * span, low)
    sum_rows = (pairs * span, wide)
    (attended,) = attend(
        forward_kernel, (ids, starts), (query, key, value), (query.shape,),
        (query_rows, key_rows, key_rows, query_rows),
    )
    _, far_o = scatter_far(grad_out, attended)
    _, across_o = scatter_near(grad_out, attended, far_o)
    upstream = project(grad_out, "o")
    halo_shape = (2, HALO, width)
    dquery, dkey, dvalue, dbefore, dafter = attend(
        backward_kernel, (ids, starts), (query, upstream, key, value),
        (query.shape, key.shape, value.shape, halo_shape, halo_shape),
        (query_rows, query_rows, key_rows, key_rows, sum_rows, sum_rows, query_rows),
    )
    _, far_q = scatter_far(normed_low, dquery)
    _, across_q = scatter_near(normed_low, dquery, far_q)
    from_next = shift(dbefore, -1)
    from_prev = shift(dafter, 1)
    block_v, far_v = scatter_far(normed_wide, dvalue)
    block_k, far_k = scatter_far(normed_wide, dkey)
    from_next, from_prev, dq, _, _ = lax.optimization_barrier(
        (from_next, from_prev, dquery, block_v, block_k)
    )
    grads = [dq]
    for side, grad in enumerate((dkey, dvalue)):
        grad = grad[HALO : HALO + tokens].astype(wide)
        grad = grad + jnp.pad(from_prev[side].astype(wide), ((0, edge), (0, 0)))
        grad = grad + jnp.pad(from_next[side].astype(wide), ((edge, 0), (0, 0)))
        grads.append(grad.astype(low))
    grad_norm = []
    for side in range(2):
        products = [dot(g, weights[name][side], (1, 1)) for name, g in zip("qkv", grads)]
        grad_norm.append(sum(products))
    _, blocks_o = scatter_line(grad_out, attended, far_o, across_o)
    _, across_v = scatter_near(normed_wide, dvalue, far_v)
    _, blocks_q = scatter_line(normed_low, dquery, far_q, across_q)
    _, across_k = scatter_near(normed_wide, dkey, far_k)
    _, blocks_v = scatter_line(normed_wide, dvalue, far_v, across_v)
    line_k, blocks_k = scatter_line(normed_wide, dkey, far_k, across_k)
    blocks_o, blocks_q, blocks_v, blocks_k = lax.optimization_barrier(
        (blocks_o, blocks_q, blocks_v, blocks_k)
    )

    def total_of(blocks):
        return sum(block.astype(wide) for block in blocks)

    out_grad = total_of(blocks_o)
    qkv_grad = jnp.stack([total_of(blocks) for blocks in (blocks_q, blocks_k, blocks_v)], axis=1)
    parts = lax.axis_size("tp")
    if parts == 2:
        total = []
        for ours in grad_norm:
            ours = ours.astype(low)
            theirs = send(ours, [(0, 1), (1, 0)], "tp")
            theirs, _ = lax.optimization_barrier((theirs, line_k))
            total.append(ours.astype(wide) + theirs.astype(wide))
        total = jnp.concatenate(total, axis=1)
        grad_input = norm_back(total, normed, inv_std).astype(low)
    else:
        share = tokens // parts
        first_row = lax.axis_index("tp") * share
        total = jnp.concatenate(grad_norm, axis=1)
        total = lax.psum_scatter(total, "tp", scatter_dimension=0, tiled=True)
        rows = lax.dynamic_slice_in_dim(normed, first_row, share, 0)
        scales = lax.dynamic_slice_in_dim(inv_std, first_row, share, 0)
        piece = norm_back(total, rows, scales).astype(low)
        grad_input = lax.all_gather(piece, "tp", axis=0, tiled=True)
    grad_input = dot(grad_input, order, (1, 1)).astype(low)
    return (grad_input, qkv_grad, out_grad)


def solution(mesh):
    placed = (P("seq", None), P("seq", None), P(), P("seq", None, "tp"), P("seq", "tp"))
    return jax.shard_map(
        per_device,
        mesh=mesh,
        in_specs=placed,
        out_specs=(P("seq", None), P("seq", None, "tp"), P("seq", "tp")),
        check_vma=False,
    )
```
